256 devices in a mesh: tm: 4 (over z_hi), space: 64 (over z_lo, x, y, core).
Axes of the slice: x: 4, y: 4, z: 8 (z_hi: 4, z_lo: 2; z = z_hi * 2 + z_lo), core: 2. Of those that a mesh axis runs over, the one named last changes fastest.
Arguments:
- states: float32 [4, 512, 64, 256], P('tm', 'space'), may hold values from -6 to 6
- conductivity: float32 [512, 64, 256], P('space'), may hold values from 0.4 to 1.6
Outputs:
- updated: float32 [4, 512, 64, 256], P('tm', 'space')
The draws below stay inside these ranges and needn't reach their ends.
All inputs are finite; a program needn't handle non-finite values.
Results may differ from the reference program's by a relative error of at most 0.0001.
Values sent between devices are 32-bit elements; how exact they have to be, the bound alone decides.
No kernel may reach another device: no remote copies, remote signals or barrier semaphores. Data moves between devices by JAX's collectives and lax.ppermute only.
A program may use at most 64 MiB of HBM per device.

```python
import math
import jax
import jax.numpy as jnp
from jax import lax

NX = 64
NY = 256
FSTEPS = 4
NZ = 512
SLICES = 4


def levels(rng, extent, split, low, top_value):
    def one(axis_at, parts):
        draws = jax.random.uniform(jax.random.fold_in(jax.random.fold_in(rng, 6), axis_at), (parts,), jnp.float32, low / len(split), top_value / len(split))
        return jnp.repeat(jnp.exp(draws), extent[axis_at] // parts).reshape((-1,) + (1,) * (len(extent) - axis_at - 1))

    factor_of = one(*split[0])
    for cut in split[1:]:
        factor_of = factor_of * one(*cut)
    return factor_of


def centred(rng, shape, width, bound, cuts=(), dtype=jnp.bfloat16):
    result = jax.random.normal(rng, shape, jnp.float32) * width
    if len(cuts) > 0:
        result = levels(rng, shape, cuts, -0.22, 0.18) * result
    return jnp.clip(result, min=-bound, max=bound).astype(dtype)


def setup_inputs(seed: int = 0) -> dict:
    streams_of = jax.random.split(jax.random.key(seed), 3)
    states = centred(streams_of[0], (SLICES, NZ, NX, NY), 1.0, 6.0, ((0, 4), (1, 64)), jnp.float32)
    conductivity = jnp.clip(jnp.exp(math.log(1.6) - 1.3862944 * jax.random.uniform(streams_of[1], (NZ, NX, NY), jnp.float32) ** levels(streams_of[1], (NZ, NX, NY), ((0, 64),), -0.2, 0.2)), 0.4, 1.6)
    return {"states": states, "conductivity": conductivity}


fine_rate = 0.1
coarsen = 4


def axis_div(field, conduct, axis):
    count = field.shape[axis]
    upper = lax.slice_in_dim(field, 1, count, axis=axis)
    lower = lax.slice_in_dim(field, 0, count - 1, axis=axis)
    upper_c = lax.slice_in_dim(conduct, 1, count, axis=axis)
    lower_c = lax.slice_in_dim(conduct, 0, count - 1, axis=axis)
    flux = 0.5 * (upper_c + lower_c) * (upper - lower)
    widths = [(0, 0), (0, 0), (0, 0)]
    widths[axis] = (1, 1)
    padded = jnp.pad(flux, widths)
    return lax.slice_in_dim(padded, 1, count + 1, axis=axis) - lax.slice_in_dim(padded, 0, count, axis=axis)


def heat_step(field, conduct, step_rate):
    div_z = axis_div(field, conduct, 0)
    div_x = axis_div(field, conduct, 1)
    div_y = axis_div(field, conduct, 2)
    return field + step_rate * (div_z + div_x + div_y)


def restrict(field):
    planes, rows, cols = field.shape
    blocks = field.reshape(planes // coarsen, coarsen, rows // coarsen, coarsen, cols // coarsen, coarsen)
    return jnp.mean(blocks, axis=(1, 3, 5))


def prolong(coarse):
    return jnp.repeat(jnp.repeat(jnp.repeat(coarse, coarsen, axis=0), coarsen, axis=1), coarsen, axis=2)


def reference(states, conductivity):
    coarse_rate = fine_rate * FSTEPS / 16.0
    coarse_conduct = restrict(conductivity)
    slices = states.shape[0]
    fine_ends = []
    olds = []
    jumps = []
    for number in range(slices):
        field = states[number]
        for turn in range(FSTEPS):
            field = heat_step(field, conductivity, fine_rate)
        fine_ends.append(field)
        coarse_old = heat_step(restrict(states[number]), coarse_conduct, coarse_rate)
        olds.append(coarse_old)
        jumps.append(restrict(field) - coarse_old)
    coarse_now = restrict(states[0])
    outputs = []
    for number in range(slices):
        coarse_new = heat_step(coarse_now, coarse_conduct, coarse_rate)
        outputs.append(fine_ends[number] + prolong(coarse_new - olds[number]))
        coarse_now = coarse_new + jumps[number]
    return jnp.stack(outputs)
```

```python
import jax
import jax.numpy as jnp
from jax import lax
from jax.experimental import pallas as pl
from jax.experimental.pallas import tpu as pltpu
from jax.sharding import PartitionSpec as P

FSTEPS = 4
COARSEN = 4
FINE_RATE = 0.1
COARSE_RATE = FINE_RATE * FSTEPS / 16.0
HALF = 4
F32 = jnp.float32
VMEM_LIMIT = 24 * 1024 * 1024


def roll_up(a, axis):
    return pltpu.roll(a, a.shape[axis] - 1, axis)


def roll_down(a, axis):
    return pltpu.roll(a, 1, axis)


def keep_faces(a, axis):
    at = lax.broadcasted_iota(jnp.int32, a.shape, axis)
    return jnp.where(at < a.shape[axis] - 1, a, 0.0)


def side_coefficients(c, scale):
    kx = keep_faces((c + roll_up(c, 0)) * scale, 0)
    ky = keep_faces((c + roll_up(c, 1)) * scale, 1)
    return kx, ky


def stencil(v, above, below, kz_above, kz_below, kx, ky):
    fx = kx * (roll_up(v, 0) - v)
    fy = ky * (roll_up(v, 1) - v)
    dz = kz_above * (above - v) - kz_below * (v - below)
    dx = fx - roll_down(fx, 0)
    dy = fy - roll_down(fy, 1)
    return v + (dz + dx + dy)


def pooling(rows, cols):
    a = lax.broadcasted_iota(jnp.int32, (rows, cols), 0)
    b = lax.broadcasted_iota(jnp.int32, (rows, cols), 1)
    if rows > cols:
        return jnp.where(a // COARSEN == b, 1.0, 0.0).astype(F32)
    return jnp.where(b // COARSEN == a, 1.0, 0.0).astype(F32)


def dot(a, b):
    return lax.dot_general(
        a, b, (((1,), (0,)), ((), ())), precision=lax.Precision.HIGHEST, preferred_element_type=F32
    )


def pooled(total):
    rows, cols = total.shape
    lanes = dot(total, pooling(cols, cols // COARSEN))
    return dot(pooling(rows // COARSEN, rows), lanes) * (1.0 / COARSEN**3)


def spread(coarse):
    rows, cols = coarse.shape
    tall = dot(pooling(rows * COARSEN, rows), coarse)
    return dot(tall, pooling(cols, cols * COARSEN))


def own_plane(par, i):
    return i + par * (7 - 2 * i)


def fast_plane(par, i):
    return i + par * (3 - 2 * i)


def slow_plane(par, i):
    return (3 - i) + par * (2 * i - 3)


def fill_coefficients(c, kx, ky, kz, lo, hi, face_lo, face_hi, scale):
    @pl.loop(lo, hi)
    def _(p):
        kx[p], ky[p] = side_coefficients(c[p], scale)

    @pl.loop(face_lo, face_hi)
    def _(p):
        kz[p] = (c[p] + c[p + 1]) * scale


def advance(src, dst, shift, kx, ky, kz, lo, hi):
    @pl.loop(lo, hi)
    def _(p):
        dst[p + shift] = stencil(src[p], src[p + 1], src[p - 1], kz[p], kz[p - 1], kx[p], ky[p])


def early_kernel(at, v, c, h, edge, fine, early, v0, c0, w1, w2, w3, kx, ky, kz):
    par = at[0]

    @pl.loop(0, 8)
    def _(i):
        v0[i] = v[own_plane(par, i)]
        c0[i] = c[own_plane(par, i)]

    @pl.loop(0, 4)
    def _(i):
        v0[8 + i] = h[fast_plane(par, i)]
        c0[8 + i] = h[4 + fast_plane(par, i)]

    scale = 0.5 * FINE_RATE
    fill_coefficients(c0, kx, ky, kz, 1, 11, 0, 11, scale)
    advance(v0, w1, 0, kx, ky, kz, 1, 11)
    advance(w1, w2, 0, kx, ky, kz, 2, 10)
    advance(w2, w3, 0, kx, ky, kz, 3, 9)
    advance(w3, fine, -4, kx, ky, kz, 4, 8)
    edge[0] = w1[1]
    edge[1] = w1[2]
    edge[2] = w2[2]
    edge[3] = w2[3]
    edge[4] = w3[3]
    edge[5] = w3[4]
    early[0] = pooled(fine[0] + fine[1] + fine[2] + fine[3])
    for b in range(2):
        early[1 + b] = pooled(v0[4 * b] + v0[4 * b + 1] + v0[4 * b + 2] + v0[4 * b + 3])
        early[3 + b] = pooled(c0[4 * b] + c0[4 * b + 1] + c0[4 * b + 2] + c0[4 * b + 3])


def late_kernel(at, v, c, g, edge, early, theirs, fine, out, v0, c0, w1, w2, w3, kx, ky, kz):
    par = at[0]

    @pl.loop(0, 4)
    def _(i):
        v0[3 - i] = g[slow_plane(par, i)]
        c0[3 - i] = g[4 + slow_plane(par, i)]

    @pl.loop(0, 2)
    def _(i):
        v0[4 + i] = v[own_plane(par, i)]

    @pl.loop(0, 5)
    def _(i):
        c0[4 + i] = c[own_plane(par, i)]

    scale = 0.5 * FINE_RATE
    fill_coefficients(c0, kx, ky, kz, 1, 8, 0, 8, scale)
    kz[3] = jnp.where(at[1] > 0, kz[3], 0.0)
    w1[5] = edge[0]
    w1[6] = edge[1]
    w2[6] = edge[2]
    w2[7] = edge[3]
    w3[7] = edge[4]
    w3[8] = edge[5]
    advance(v0, w1, 0, kx, ky, kz, 1, 5)
    advance(w1, w2, 0, kx, ky, kz, 2, 6)
    advance(w2, w3, 0, kx, ky, kz, 3, 7)
    advance(w3, fine, -4, kx, ky, kz, 4, 8)
    out[0] = pooled(fine[0] + fine[1] + fine[2] + fine[3])
    out[1] = early[0]
    out[2] = theirs[0]
    out[3] = early[1]
    out[4] = early[2]
    out[5] = theirs[2]
    out[6] = early[3]
    out[7] = early[4]
    out[8] = theirs[4]


def final_kernel(at, near, own, other, far, cc, lower, upper, out):
    par, slow_ok, fast_ok, slice_at = at[0], at[1], at[2], at[3]
    scale = 0.5 * COARSE_RATE
    kx, ky, kz = {}, {}, {}
    for p in range(-2, 4):
        kx[p], ky[p] = side_coefficients(cc[p + 3], scale)
    for p in range(-3, 4):
        kz[p] = (cc[p + 3] + cc[p + 4]) * scale
    kz[-1] = jnp.where(slow_ok > 0, kz[-1], 0.0)
    kz[3] = jnp.where(fast_ok > 0, kz[3], 0.0)

    def pick(which, field, p):
        mine, flipped = near[field, p + 3], other[field, 6 - p]
        return jnp.where((par == 0) == (which == 1), mine, flipped)

    def gate(level, a):
        return jnp.where(slice_at >= level, a, 0.0)

    def grow(d, lo, hi):
        return {
            p: stencil(d[p], d[p + 1], d[p - 1], kz[p], kz[p - 1], kx[p], ky[p]) for p in range(lo, hi)
        }

    d = {p: gate(3, far[0, p + 3] - pick(2, 1, p)) for p in range(-3, 5)}
    u = grow(d, -2, 4)
    d = {p: u[p] + gate(2, pick(2, 0, p) - pick(1, 1, p)) for p in range(-2, 4)}
    u = grow(d, -1, 3)
    d = {p: u[p] + gate(1, pick(1, 0, p) - own[1, p + 3]) for p in range(-1, 3)}
    u = grow(d, 0, 2)
    for half, fine in ((0, lower), (1, upper)):
        change = spread(u[half])

        @pl.loop(0, 4)
        def _(i):
            out[own_plane(par, 4 * half + i)] = fine[i] + change


def call(kernel, outs, scratch, flops, count):
    return pl.pallas_call(
        kernel,
        out_shape=[jax.ShapeDtypeStruct(s, F32) for s in outs],
        in_specs=[pl.BlockSpec(memory_space=pltpu.SMEM)]
        + [pl.BlockSpec(memory_space=pltpu.VMEM)] * (count - 1),
        out_specs=[pl.BlockSpec(memory_space=pltpu.VMEM)] * len(outs),
        scratch_shapes=[pltpu.VMEM(s, F32) for s in scratch],
        compiler_params=pltpu.CompilerParams(vmem_limit_bytes=VMEM_LIMIT),
        cost_estimate=pl.CostEstimate(flops=flops, bytes_accessed=flops // 4, transcendentals=0),
    )


def per_device(states, conductivity):
    v, c = states[0], conductivity
    planes, rows, cols = v.shape
    plane = (rows, cols)
    small = (rows // COARSEN, cols // COARSEN)
    k, n = lax.axis_index("space"), lax.axis_index("tm")
    count, slices = lax.axis_size("space"), lax.axis_size("tm")
    par = k % 2
    mate = k + 1 - 2 * par
    inside = lambda i: ((i != 0) & (i != count - 1)).astype(jnp.int32)
    at = jnp.stack([par, inside(k), inside(mate), n]).astype(jnp.int32)

    slow_pairs = [(i, i + 1) for i in range(1, count - 1, 2)]
    slow_pairs += [(b, a) for a, b in slow_pairs]
    fast_pairs = [(i, i ^ 1) for i in range(count)]
    slow = lambda x: lax.ppermute(x, "space", slow_pairs)
    fast = lambda x: lax.ppermute(x, "space", fast_pairs)

    half = lambda a, side: lax.dynamic_slice_in_dim(a, side * HALF, HALF, 0)
    from_slow = slow(jnp.concatenate([half(v, par), half(c, par)]))
    from_fast = fast(jnp.concatenate([half(v, 1 - par), half(c, 1 - par)]))

    edge, upper, early = call(
        early_kernel,
        [(6,) + plane, (4,) + plane, (5,) + small],
        [(12,) + plane] * 8,
        12_000_000,
        4,
    )(at, v, c, from_fast)
    theirs = fast(early)
    lower, coarse = call(
        late_kernel,
        [(4,) + plane, (9,) + small],
        [(10,) + plane] * 8,
        6_000_000,
        7,
    )(at, v, c, from_slow, edge, early, theirs)
    beyond = slow(coarse)
    mate_late = fast(jnp.concatenate([coarse[:1], beyond]))

    def line(mine, mate, at_mine, at_beyond, at_mate):
        return jnp.stack(
            [beyond[at_beyond + 2], beyond[at_beyond + 1], beyond[at_beyond], mine[0], mine[1], mate[0], mate[1]]
            + [mate_late[1 + at_beyond + i] for i in range(3)]
        )

    ends = line((coarse[0], coarse[1]), (theirs[0], mate_late[0]), 0, 0, 0)
    starts = line((early[1], early[2]), (theirs[2], theirs[1]), 0, 3, 0)
    cc = line((early[3], early[4]), (theirs[4], theirs[3]), 0, 6, 0)
    own = jnp.stack([ends, starts])

    pairs = []
    for i in range(count):
        step = 1 + i % 2
        pairs += [(s * count + i, (s + step) * count + i) for s in range(slices - step)]
    near = lax.ppermute(own, ("tm", "space"), pairs)
    far = lax.ppermute(own, "tm", [(0, slices - 1)])
    other = fast(near)
    (result,) = call(final_kernel, [(planes,) + plane], [], 1_000_000, 8)(
        at, near, own, other, far, cc, lower, upper
    )
    return result[None]


def solution(mesh):
    return jax.shard_map(
        per_device,
        mesh=mesh,
        in_specs=(P("tm", "space", None, None), P("space", None, None)),
        out_specs=P("tm", "space", None, None),
        check_vma=False,
    )
```

```python
import jax
import jax.numpy as jnp
from jax import lax
from jax.experimental import pallas as pl
from jax.experimental.pallas import tpu as pltpu
from jax.sharding import PartitionSpec as P


FSTEPS = 4
COARSEN = 4
FINE_RATE = 0.1
COARSE_RATE = FINE_RATE * FSTEPS / 16.0
HALF = 4
F32 = jnp.float32
BF16 = jnp.bfloat16
VMEM_LIMIT = 24 * 1024 * 1024
PACK_LIMIT = VMEM_LIMIT
LANES = 128
ROWS = 64
TOP = 8
PADDED = 80
UNROLL = True
CHUNK = 8


def own_plane(par, i):
    return i + par * (7 - 2 * i)


def fast_plane(par, i):
    return i + par * (3 - 2 * i)


def slow_plane(par, i):
    return (3 - i) + par * (2 * i - 3)


def rows_of(ref, p, h, shift=0):
    return ref[p, h, TOP + shift : TOP + ROWS + shift, :]


def put(ref, p, plane):
    for h in range(2):
        ref[p, h, TOP : TOP + ROWS, :] = plane[:, h * LANES : (h + 1) * LANES]


def blank_margins(ref, planes):
    for p in range(planes):
        for h in range(2):
            ref[p, h, 0:TOP, :] = jnp.zeros((TOP, LANES), F32)
            ref[p, h, TOP + ROWS : PADDED, :] = jnp.zeros((TOP, LANES), F32)


def mirror_margins(ref, p):
    for h in range(2):
        ref[p, h, TOP - 1 : TOP, :] = -ref[p, h, TOP : TOP + 1, :]
        ref[p, h, TOP + ROWS : TOP + ROWS + 1, :] = -ref[p, h, TOP + ROWS - 1 : TOP + ROWS, :]


def lane_turns(a0, a1):
    at = lax.broadcasted_iota(jnp.int32, a0.shape, 1)
    up0, up1 = pltpu.roll(a0, LANES - 1, 1), pltpu.roll(a1, LANES - 1, 1)
    down0, down1 = pltpu.roll(a0, 1, 1), pltpu.roll(a1, 1, 1)
    return (jnp.where(at == LANES - 1, up1, up0), up1), (down0, jnp.where(at == 0, down0, down1)), at


def fill_faces(c, kz, lo, hi, scale, unroll):
    @pl.loop(lo, hi, unroll=unroll)
    def _(p):
        for h in range(2):
            kz[p, h] = (rows_of(c, p, h) + rows_of(c, p + 1, h)) * scale


def fill_coefficients(c, kz, k, lo, hi, scale, unroll):
    @pl.loop(lo, hi, unroll=unroll)
    def _(p):
        a0, a1 = rows_of(c, p, 0), rows_of(c, p, 1)
        (up0, up1), (down0, down1), at = lane_turns(a0, a1)
        up1 = jnp.where(at == LANES - 1, -a1, up1)
        down0 = jnp.where(at == 0, -a0, down0)
        for h, a, up, down in ((0, a0, up0, down0), (1, a1, up1, down1)):
            kxu = (a + rows_of(c, p, h, 1)) * scale
            kxd = (a + rows_of(c, p, h, -1)) * scale
            kyu = (a + up) * scale
            kyd = (a + down) * scale
            k[p, 0, h] = 1.0 - ((kxu + kxd) + (kyu + kyd) + (kz[p, h] + kz[p - 1, h]))
            k[p, 1, h] = kxu
            k[p, 2, h] = kxd
            k[p, 3, h] = kyu
            k[p, 4, h] = kyd


def advance(src, store, kz, k, lo, hi, unroll, shift=0):
    at = lax.broadcasted_iota(jnp.int32, (CHUNK, LANES), 1)

    def some(p):
        q = p - shift
        made = []
        for r in range(0, ROWS, CHUNK):
            cut = lambda ref, i, h, s=0: ref[i, h, TOP + r + s : TOP + r + s + CHUNK, :]
            w = lambda i, h: k[q, i, h, r : r + CHUNK, :]
            v = [cut(src, p, h) for h in range(2)]
            up = [pltpu.roll(v[h], LANES - 1, 1) for h in range(2)]
            down = [pltpu.roll(v[h], 1, 1) for h in range(2)]
            up = [jnp.where(at == LANES - 1, up[1], up[0]), up[1]]
            down = [down[0], jnp.where(at == 0, down[0], down[1])]
            for h in range(2):
                a = w(0, h) * v[h]
                b = kz[q, h, r : r + CHUNK] * cut(src, p + 1, h) + kz[q - 1, h, r : r + CHUNK] * cut(src, p - 1, h)
                d = w(1, h) * cut(src, p, h, 1) + w(2, h) * cut(src, p, h, -1)
                e = w(3, h) * up[h] + w(4, h) * down[h]
                made.append((r, h, (a + b) + (d + e)))
        return made

    @pl.loop(lo, hi, unroll=unroll)
    def _(p):
        for r, h, a in some(p):
            store(p, h, r, a)


def into(ref):
    def store(p, h, r, a):
        ref[p, h, TOP + r : TOP + r + CHUNK, :] = a

    return store


def into_fine(ref, shift):
    def store(p, h, r, a):
        ref[p - shift, h, r : r + CHUNK, :] = a

    return store


def block_sums(ref, first, top):
    parts = []
    for side in range(2):
        for h in range(2):
            total = None
            for p in range(first, first + COARSEN):
                for r in range(COARSEN):
                    term = ref[p, h, pl.ds(top + 32 * side + r, 8, stride=COARSEN), :]
                    total = term if total is None else total + term
            parts.append(total)
    return jnp.concatenate(parts, axis=1)


def mxu(a, b):
    return lax.dot_general(a, b, (((1,), (0,)), ((), ())), preferred_element_type=F32)


def split_dot(a, b):
    high = a.astype(BF16)
    low = (a - high.astype(F32)).astype(BF16)
    return mxu(high, b) + mxu(low, b)


def pooled(sums, pool):
    return split_dot(sums, pool) * (1.0 / COARSEN**3)


def pack_kernel(at, v, c, near_slow, near_fast, sems):
    par = at[0]
    copies = []
    for s, (ref, side) in enumerate(((near_slow, par), (near_fast, 1 - par))):
        for f, src in enumerate((v, c)):
            copies.append(
                pltpu.make_async_copy(
                    src.at[pl.ds(side * HALF, HALF)], ref.at[pl.ds(f * HALF, HALF)], sems.at[2 * s + f]
                )
            )
    for copy in copies:
        copy.start()
    for copy in copies:
        copy.wait()


def put_own(par, near_slow, near_fast, field, coefficient):
    @pl.loop(0, 4)
    def _(i):
        for base, ref in ((0, near_slow), (4, near_fast)):
            put(field, base + i, ref[fast_plane(par, i)])
            put(coefficient, base + i, ref[HALF + fast_plane(par, i)])


def coarse_kernel(at, near_slow, near_fast, pool, out, v0, c0):
    put_own(at[0], near_slow, near_fast, v0, c0)
    sums = [block_sums(ref, 4 * b, TOP) for ref in (v0, c0) for b in range(2)]
    res = pooled(jnp.concatenate(sums, axis=0), pool[...])
    for i in range(4):
        out[i] = res[8 * i : 8 * i + 8]


def early_kernel(at, near_slow, near_fast, h, pool, own, theirs, a, b, kz, k, fine, end, starts, c0):
    par = at[0]
    blank_margins(a, 12)
    blank_margins(b, 12)
    put_own(par, near_slow, near_fast, a, c0)

    @pl.loop(0, 4)
    def _(i):
        put(a, 8 + i, h[fast_plane(par, i)])
        put(c0, 8 + i, h[HALF + fast_plane(par, i)])

    for i in range(12):
        mirror_margins(c0, i)
    scale = 0.5 * FINE_RATE
    fill_faces(c0, kz, 0, 11, scale, UNROLL)
    fill_coefficients(c0, kz, k, 1, 11, scale, UNROLL)
    advance(a, into(b), kz, k, 1, 11, UNROLL)
    advance(b, into(a), kz, k, 2, 10, UNROLL)
    advance(a, into(b), kz, k, 3, 9, UNROLL)
    advance(b, into_fine(fine, 4), kz, k, 4, 8, UNROLL)
    end[0] = pooled(block_sums(fine, 0, 0), pool[...])
    starts[0] = own[0]
    starts[1] = own[1]
    starts[2] = theirs[1]


def late_kernel(at, near_slow, g, a, b, kz, k, pool, fine, end, v0, c0, w0, kl, kzl):
    par = at[0]
    blank_margins(v0, 10)
    blank_margins(w0, 10)

    @pl.loop(0, 4)
    def _(i):
        put(v0, 3 - i, g[slow_plane(par, i)])
        put(c0, 3 - i, g[HALF + slow_plane(par, i)])

    for i in range(2):
        put(v0, 4 + i, near_slow[fast_plane(par, i)])
        put(c0, 4 + i, near_slow[HALF + fast_plane(par, i)])
    for i in range(6):
        mirror_margins(c0, i)
    scale = 0.5 * FINE_RATE
    fill_faces(c0, kzl, 0, 5, scale, True)
    for h in range(2):
        kzl[3, h] = jnp.where(at[1] > 0, kzl[3, h], 0.0)
    fill_coefficients(c0, kzl, kl, 1, 5, scale, True)
    advance(v0, into(w0), kzl, kl, 1, 5, True)
    for h in range(2):
        w0[5, h] = b[1, h]
        w0[6, h] = b[2, h]
    advance(w0, into(v0), kzl, kl, 2, 5, True)
    advance(w0, into(v0), kz, k, 5, 6, True, 4)
    for h in range(2):
        v0[6, h] = a[2, h]
        v0[7, h] = a[3, h]
    advance(v0, into(w0), kzl, kl, 3, 5, True)
    advance(v0, into(w0), kz, k, 5, 7, True, 4)
    for h in range(2):
        w0[7, h] = b[3, h]
        w0[8, h] = b[4, h]
    advance(w0, into_fine(fine, 4), kzl, kl, 4, 5, True)
    advance(w0, into_fine(fine, 4), kz, k, 5, 8, True, 4)
    end[0] = pooled(block_sums(fine, 0, 0), pool[...])


def row_turns(a):
    other = pltpu.roll(a, LANES // 2, 1)
    row = lax.broadcasted_iota(jnp.int32, a.shape, 0)
    up = jnp.where(row == 7, pltpu.roll(other, 7, 0), pltpu.roll(a, 7, 0))
    down = jnp.where(row == 0, pltpu.roll(other, 1, 0), pltpu.roll(a, 1, 0))
    return up, down


def weights_kernel(at, cc, kz, k):
    scale = 0.5 * COARSE_RATE
    row = lax.broadcasted_iota(jnp.int32, (8, LANES), 0)
    lane = lax.broadcasted_iota(jnp.int32, (8, LANES), 1)
    left = lane < LANES // 2
    up_ok = jnp.where(left | (row < 7), scale, 0.0)
    down_ok = jnp.where(left & (row == 0), 0.0, scale)
    right_ok = jnp.where(lane % (LANES // 2) == LANES // 2 - 1, 0.0, scale)
    left_ok = jnp.where(lane % (LANES // 2) == 0, 0.0, scale)
    faces = [(cc[i] + cc[i + 1]) * scale for i in range(7)]
    faces[2] = jnp.where(at[1] > 0, faces[2], 0.0)
    faces[6] = jnp.where(at[2] > 0, faces[6], 0.0)
    for i in range(7):
        kz[i] = faces[i]
    for i in range(6):
        c = cc[i + 1]
        up, down = row_turns(c)
        kxu, kxd = (c + up) * up_ok, (c + down) * down_ok
        kyu = (c + pltpu.roll(c, LANES - 1, 1)) * right_ok
        kyd = (c + pltpu.roll(c, 1, 1)) * left_ok
        k[i, 0] = 1.0 - ((kxu + kxd) + (kyu + kyd) + (faces[i] + faces[i + 1]))
        k[i, 1] = kxu
        k[i, 2] = kxd
        k[i, 3] = kyu
        k[i, 4] = kyd


def final_kernel(at, near, far, other, kz, k, spread, tall, lower, upper, out):
    par, slice_at = at[0], at[3]

    def pick(level, p):
        return jnp.where((par == 1) == (level == 1), near[p + 2], other[5 - p])

    def gate(level, a):
        return jnp.where(slice_at >= level, a, 0.0)

    def grow(d, lo, hi):
        u = {}
        for p in range(lo, hi):
            v = d[p]
            up, down = row_turns(v)
            w = [k[p + 2, i] for i in range(5)]
            x = w[1] * up + w[2] * down
            y = w[3] * pltpu.roll(v, LANES - 1, 1) + w[4] * pltpu.roll(v, 1, 1)
            u[p] = (w[0] * v + (kz[p + 3] * d[p + 1] + kz[p + 2] * d[p - 1])) + (x + y)
        return u

    d = {p: gate(3, jnp.where(par == 1, far[p + 3], other[14 - p])) for p in range(-3, 5)}
    u = grow(d, -2, 4)
    d = {p: u[p] + gate(2, pick(2, p)) for p in range(-2, 4)}
    u = grow(d, -1, 3)
    d = {p: u[p] + gate(1, pick(1, p)) for p in range(-1, 3)}
    u = grow(d, 0, 2)
    wide = split_dot(jnp.concatenate([u[0], u[1]], axis=0), spread[...])
    high = wide.astype(BF16)
    low = (wide - high.astype(F32)).astype(BF16)
    change = mxu(tall[...], high) + mxu(tall[...], low)
    for half, fine in ((0, lower), (1, upper)):

        @pl.loop(0, 4)
        def _(i):
            at_plane = own_plane(par, 4 * half + i)
            for side in range(2):
                for h in range(2):
                    rows = slice(32 * side, 32 * side + 32)
                    cut = change[32 * half : 32 * half + 32, 256 * side + LANES * h : 256 * side + LANES * (h + 1)]
                    out[at_plane, rows, LANES * h : LANES * (h + 1)] = fine[i, h, rows] + cut


def call(kernel, outs, scratch, flops, count):
    return pl.pallas_call(
        kernel,
        out_shape=[jax.ShapeDtypeStruct(s, F32) for s in outs],
        in_specs=[pl.BlockSpec(memory_space=pltpu.SMEM)]
        + [pl.BlockSpec(memory_space=pltpu.VMEM)] * (count - 1),
        out_specs=[pl.BlockSpec(memory_space=pltpu.VMEM)] * len(outs),
        scratch_shapes=[pltpu.VMEM(s, F32) for s in scratch],
        compiler_params=pltpu.CompilerParams(vmem_limit_bytes=VMEM_LIMIT),
        cost_estimate=pl.CostEstimate(flops=flops, bytes_accessed=flops // 4, transcendentals=0),
    )


def matches(rows, cols, by_row):
    r = lax.broadcasted_iota(jnp.int32, (rows, cols), 0)
    c = lax.broadcasted_iota(jnp.int32, (rows, cols), 1)
    return (r // COARSEN == c if by_row else c // COARSEN == r).astype(BF16)


def per_device(states, conductivity):
    return iteration(states[0], conductivity)[None]


def iteration(v, c):
    planes, rows, cols = v.shape
    plane = (rows, cols)
    wide, padded, block = (2, ROWS, LANES), (2, PADDED, LANES), (8, LANES)
    k, n = lax.axis_index("space"), lax.axis_index("tm")
    count, slices = lax.axis_size("space"), lax.axis_size("tm")
    par = k % 2
    mate = k + 1 - 2 * par
    inside = lambda i: ((i != 0) & (i != count - 1)).astype(jnp.int32)
    at = jnp.stack([par, inside(k), inside(mate), n]).astype(jnp.int32)

    slow_pairs = [(i, i + 1) for i in range(1, count - 1, 2)]
    slow_pairs += [(b, a) for a, b in slow_pairs]
    fast_pairs = [(i, i ^ 1) for i in range(count)]
    slow = lambda x: lax.ppermute(x, "space", slow_pairs)
    fast = lambda x: lax.ppermute(x, "space", fast_pairs)

    half = (2 * HALF,) + plane
    near_slow, near_fast = pl.pallas_call(
        pack_kernel,
        out_shape=[jax.ShapeDtypeStruct(half, F32)] * 2,
        in_specs=[pl.BlockSpec(memory_space=pltpu.SMEM)] + [pl.BlockSpec(memory_space=pltpu.HBM)] * 2,
        out_specs=[pl.BlockSpec(memory_space=pltpu.VMEM)] * 2,
        scratch_shapes=[pltpu.SemaphoreType.DMA((4,))],
        compiler_params=pltpu.CompilerParams(vmem_limit_bytes=PACK_LIMIT),
    )(at, *(pltpu.with_memory_space_constraint(x, pltpu.HBM) for x in (v, c)))
    from_slow = slow(near_slow)
    from_fast = fast(near_fast)
    pool = matches(512, LANES, True)
    spread = matches(LANES, 512, False)
    tall = matches(64, 16, True)

    (own,) = call(coarse_kernel, [(4,) + block], [(8,) + padded] * 2, 1_000_000, 4)(at, near_slow, near_fast, pool)
    theirs = fast(own)
    a, b, kz, kk, upper, end, starts = call(
        early_kernel,
        [(12,) + padded, (12,) + padded, (11,) + wide, (11, 5) + wide, (4,) + wide, (1,) + block, (3,) + block],
        [(12,) + padded],
        8_000_000,
        7,
    )(at, near_slow, near_fast, from_fast, pool, own, theirs)
    their_end = fast(end)
    following = lax.ppermute(starts, "tm", [(i + 1, i) for i in range(slices - 1)])
    lower, first_end = call(
        late_kernel,
        [(4,) + wide, (1,) + block],
        [(10,) + padded] * 3 + [(5, 5) + wide, (5,) + wide],
        4_000_000,
        8,
    )(at, near_slow, from_slow, a, b, kz, kk, pool)
    gaps = jnp.concatenate([first_end, end, their_end]) - following
    beyond = slow(jnp.concatenate([gaps, own[2:], theirs[3:]]))
    late = fast(jnp.concatenate([gaps[:1], beyond[:4]]))

    line = jnp.stack(
        [beyond[2], beyond[1], beyond[0], gaps[0], gaps[1], gaps[2], late[0], late[1], late[2], late[3]]
    )
    pairs = []
    for i in range(count):
        step = 2 - i % 2
        pairs += [(s * count + i, (s + step) * count + i) for s in range(slices - step)]
    near = lax.ppermute(line[1:9], ("tm", "space"), pairs)
    far = lax.ppermute(line, ("tm", "space"), [(i, (slices - 1) * count + i) for i in range(1, count, 2)])
    cc = jnp.stack([beyond[5], beyond[4], beyond[3], own[2], own[3], theirs[3], theirs[2], late[4]])
    ckz, ck = call(weights_kernel, [(7,) + block, (6, 5) + block], [], 100_000, 2)(at, cc)
    other = fast(jnp.concatenate([near, far]))
    (result,) = call(final_kernel, [(planes,) + plane], [], 1_000_000, 10)(
        at, near, far, other, ckz, ck, spread, tall, lower, upper
    )
    return result


def solution(mesh):
    return jax.shard_map(
        per_device,
        mesh=mesh,
        in_specs=(P("tm", "space", None, None), P("space", None, None)),
        out_specs=P("tm", "space", None, None),
        check_vma=False,
    )
```

```python
import jax
import jax.numpy as jnp
from jax import lax
from jax.experimental import pallas as pl
from jax.experimental.pallas import tpu as pltpu
from jax.sharding import PartitionSpec as P


FSTEPS = 4
COARSEN = 4
FINE_RATE = 0.1
COARSE_RATE = FINE_RATE * FSTEPS / 16.0
HALF = 4
F32 = jnp.float32
BF16 = jnp.bfloat16
VMEM_LIMIT = 24 * 1024 * 1024
LANES = 128
ROWS = 64
TOP = 8
PADDED = 80
UNROLL = True
CHUNK = 8


def fast_plane(par, i):
    return i + par * (3 - 2 * i)


def slow_plane(par, i):
    return (3 - i) + par * (2 * i - 3)


def rows_of(ref, p, h, shift=0):
    return ref[p, h, TOP + shift : TOP + ROWS + shift, :]


def put(ref, p, plane):
    for h in range(2):
        ref[p, h, TOP : TOP + ROWS, :] = plane[:, h * LANES : (h + 1) * LANES]


def blank_margins(ref, planes):
    for p in range(planes):
        for h in range(2):
            ref[p, h, 0:TOP, :] = jnp.zeros((TOP, LANES), F32)
            ref[p, h, TOP + ROWS : PADDED, :] = jnp.zeros((TOP, LANES), F32)


def mirror_margins(ref, p):
    for h in range(2):
        ref[p, h, TOP - 1 : TOP, :] = -ref[p, h, TOP : TOP + 1, :]
        ref[p, h, TOP + ROWS : TOP + ROWS + 1, :] = -ref[p, h, TOP + ROWS - 1 : TOP + ROWS, :]


def lane_turns(a0, a1):
    at = lax.broadcasted_iota(jnp.int32, a0.shape, 1)
    up0, up1 = pltpu.roll(a0, LANES - 1, 1), pltpu.roll(a1, LANES - 1, 1)
    down0, down1 = pltpu.roll(a0, 1, 1), pltpu.roll(a1, 1, 1)
    return (jnp.where(at == LANES - 1, up1, up0), up1), (down0, jnp.where(at == 0, down0, down1)), at


def fill_faces(c, kz, lo, hi, scale, unroll):
    @pl.loop(lo, hi, unroll=unroll)
    def _(p):
        for h in range(2):
            kz[p, h] = (rows_of(c, p, h) + rows_of(c, p + 1, h)) * scale


def fill_coefficients(c, kz, k, lo, hi, scale, unroll):
    @pl.loop(lo, hi, unroll=unroll)
    def _(p):
        a0, a1 = rows_of(c, p, 0), rows_of(c, p, 1)
        (up0, up1), (down0, down1), at = lane_turns(a0, a1)
        up1 = jnp.where(at == LANES - 1, -a1, up1)
        down0 = jnp.where(at == 0, -a0, down0)
        for h, a, up, down in ((0, a0, up0, down0), (1, a1, up1, down1)):
            kxu = (a + rows_of(c, p, h, 1)) * scale
            kxd = (a + rows_of(c, p, h, -1)) * scale
            kyu = (a + up) * scale
            kyd = (a + down) * scale
            k[p, 0, h] = 1.0 - ((kxu + kxd) + (kyu + kyd) + (kz[p, h] + kz[p - 1, h]))
            k[p, 1, h] = kxu
            k[p, 2, h] = kxd
            k[p, 3, h] = kyu
            k[p, 4, h] = kyd


def advance(src, store, kz, k, lo, hi, unroll, shift=0):
    at = lax.broadcasted_iota(jnp.int32, (CHUNK, LANES), 1)

    def some(p):
        q = p - shift
        made = []
        for r in range(0, ROWS, CHUNK):
            cut = lambda ref, i, h, s=0: ref[i, h, TOP + r + s : TOP + r + s + CHUNK, :]
            w = lambda i, h: k[q, i, h, r : r + CHUNK, :]
            v = [cut(src, p, h) for h in range(2)]
            up = [pltpu.roll(v[h], LANES - 1, 1) for h in range(2)]
            down = [pltpu.roll(v[h], 1, 1) for h in range(2)]
            up = [jnp.where(at == LANES - 1, up[1], up[0]), up[1]]
            down = [down[0], jnp.where(at == 0, down[0], down[1])]
            for h in range(2):
                a = w(0, h) * v[h]
                b = kz[q, h, r : r + CHUNK] * cut(src, p + 1, h) + kz[q - 1, h, r : r + CHUNK] * cut(src, p - 1, h)
                d = w(1, h) * cut(src, p, h, 1) + w(2, h) * cut(src, p, h, -1)
                e = w(3, h) * up[h] + w(4, h) * down[h]
                made.append((r, h, (a + b) + (d + e)))
        return made

    @pl.loop(lo, hi, unroll=unroll)
    def _(p):
        for r, h, a in some(p):
            store(p, h, r, a)


def into(ref):
    def store(p, h, r, a):
        ref[p, h, TOP + r : TOP + r + CHUNK, :] = a

    return store


def into_fine(ref, shift):
    def store(p, h, r, a):
        ref[p - shift, h, r : r + CHUNK, :] = a

    return store


def block_sums(ref, first, top):
    parts = []
    for side in range(2):
        for h in range(2):
            total = None
            for p in range(first, first + COARSEN):
                for r in range(COARSEN):
                    term = ref[p, h, pl.ds(top + 32 * side + r, 8, stride=COARSEN), :]
                    total = term if total is None else total + term
            parts.append(total)
    return jnp.concatenate(parts, axis=1)


def mxu(a, b):
    return lax.dot_general(a, b, (((1,), (0,)), ((), ())), preferred_element_type=F32)


def split_dot(a, b):
    high = a.astype(BF16)
    low = (a - high.astype(F32)).astype(BF16)
    return mxu(high, b) + mxu(low, b)


def pooled(sums, pool):
    return split_dot(sums, pool) * (1.0 / COARSEN**3)


def matches(rows, cols, by_row):
    r = lax.broadcasted_iota(jnp.int32, (rows, cols), 0)
    c = lax.broadcasted_iota(jnp.int32, (rows, cols), 1)
    same = r // COARSEN == c if by_row else c // COARSEN == r
    return jnp.where(same, 1.0, 0.0).astype(BF16)


def pack_kernel(at, v, c, near_slow, near_fast, pool, spread, tall, sems):
    par = at[0]
    copies = []
    for s, (ref, side) in enumerate(((near_slow, par), (near_fast, 1 - par))):
        for f, src in enumerate((v, c)):
            copies.append(
                pltpu.make_async_copy(
                    src.at[pl.ds(side * HALF, HALF)], ref.at[pl.ds(f * HALF, HALF)], sems.at[2 * s + f]
                )
            )
    for copy in copies:
        copy.start()
    pool[...] = matches(*pool.shape, True)
    spread[...] = matches(*spread.shape, False)
    tall[...] = matches(*tall.shape, True)
    for copy in copies:
        copy.wait()


def put_own(par, near_slow, near_fast, field, coefficient):
    @pl.loop(0, 4)
    def _(i):
        for base, ref in ((0, near_slow), (4, near_fast)):
            put(field, base + i, ref[fast_plane(par, i)])
            put(coefficient, base + i, ref[HALF + fast_plane(par, i)])


def coarse_kernel(at, near_slow, near_fast, pool, out, v0, c0):
    put_own(at[0], near_slow, near_fast, v0, c0)
    sums = [block_sums(ref, 4 * b, TOP) for ref in (v0, c0) for b in range(2)]
    res = pooled(jnp.concatenate(sums, axis=0), pool[...])
    for i in range(4):
        out[i] = res[8 * i : 8 * i + 8]


def early_kernel(at, near_slow, near_fast, h, pool, a, b, kz, k, fine, end, c0):
    par = at[0]
    blank_margins(a, 12)
    blank_margins(b, 12)
    put_own(par, near_slow, near_fast, a, c0)

    @pl.loop(0, 4)
    def _(i):
        put(a, 8 + i, h[fast_plane(par, i)])
        put(c0, 8 + i, h[HALF + fast_plane(par, i)])

    for i in range(12):
        mirror_margins(c0, i)
    scale = 0.5 * FINE_RATE
    fill_faces(c0, kz, 0, 11, scale, UNROLL)
    fill_coefficients(c0, kz, k, 1, 11, scale, UNROLL)
    advance(a, into(b), kz, k, 1, 11, UNROLL)
    advance(b, into(a), kz, k, 2, 10, UNROLL)
    advance(a, into(b), kz, k, 3, 9, UNROLL)
    advance(b, into_fine(fine, 4), kz, k, 4, 8, UNROLL)
    end[0] = pooled(block_sums(fine, 0, 0), pool[...])


def row_turns(a):
    other = pltpu.roll(a, LANES // 2, 1)
    row = lax.broadcasted_iota(jnp.int32, a.shape, 0)
    up = jnp.where(row == 7, pltpu.roll(other, 7, 0), pltpu.roll(a, 7, 0))
    down = jnp.where(row == 0, pltpu.roll(other, 1, 0), pltpu.roll(a, 1, 0))
    return up, down


def coarse_masks():
    scale = 0.5 * COARSE_RATE
    row = lax.broadcasted_iota(jnp.int32, (8, LANES), 0)
    lane = lax.broadcasted_iota(jnp.int32, (8, LANES), 1)
    left = lane < LANES // 2
    up = jnp.where(left | (row < 7), scale, 0.0)
    down = jnp.where(left & (row == 0), 0.0, scale)
    right = jnp.where(lane % (LANES // 2) == LANES // 2 - 1, 0.0, scale)
    before = jnp.where(lane % (LANES // 2) == 0, 0.0, scale)
    return up, down, right, before


def coarse_weights(c, faces, masks):
    up, down = row_turns(c)
    kxu, kxd = (c + up) * masks[0], (c + down) * masks[1]
    kyu = (c + pltpu.roll(c, LANES - 1, 1)) * masks[2]
    kyd = (c + pltpu.roll(c, 1, 1)) * masks[3]
    return 1.0 - ((kxu + kxd) + (kyu + kyd) + faces), kxu, kxd, kyu, kyd


def coarse_step(v, above, below, face_above, face_below, w):
    up, down = row_turns(v)
    x = w[1] * up + w[2] * down
    y = w[3] * pltpu.roll(v, LANES - 1, 1) + w[4] * pltpu.roll(v, 1, 1)
    return (w[0] * v + (face_above * above + face_below * below)) + (x + y)


def late_kernel(
    at, near_slow, g, a, b, kz, k, pool, own, theirs, end, mate_end, fine, out, before, v0, c0, w0, kl, kzl
):
    par = at[0]
    blank_margins(v0, 10)
    blank_margins(w0, 10)

    @pl.loop(0, 4)
    def _(i):
        put(v0, 3 - i, g[slow_plane(par, i)])
        put(c0, 3 - i, g[HALF + slow_plane(par, i)])

    for i in range(2):
        put(v0, 4 + i, near_slow[fast_plane(par, i)])
        put(c0, 4 + i, near_slow[HALF + fast_plane(par, i)])
    for i in range(6):
        mirror_margins(c0, i)
    beyond = pooled(jnp.concatenate([block_sums(v0, 0, TOP), block_sums(c0, 0, TOP)], axis=0), pool[...])
    start = [beyond[:8], own[0], own[1], theirs[1], theirs[0]]
    cc = [beyond[8:], own[2], own[3], theirs[3], theirs[2]]
    faces = [(cc[i] + cc[i + 1]) * (0.5 * COARSE_RATE) for i in range(4)]
    faces[0] = jnp.where(at[1] > 0, faces[0], 0.0)
    masks = coarse_masks()
    before[0] = start[0]
    stepped = []
    for i in range(1, 4):
        w = coarse_weights(cc[i], faces[i] + faces[i - 1], masks)
        step = coarse_step(start[i], start[i + 1], start[i - 1], faces[i], faces[i - 1], w)
        stepped.append(jnp.where(at[3] > 0, step, 0.0))
        out[2 + i] = cc[i]
    out[1] = end[0] - stepped[1]
    out[2] = mate_end[0] - stepped[2]
    scale = 0.5 * FINE_RATE
    fill_faces(c0, kzl, 0, 5, scale, True)
    for h in range(2):
        kzl[3, h] = jnp.where(at[1] > 0, kzl[3, h], 0.0)
    fill_coefficients(c0, kzl, kl, 1, 5, scale, True)
    advance(v0, into(w0), kzl, kl, 1, 5, True)
    for h in range(2):
        w0[5, h] = b[1, h]
        w0[6, h] = b[2, h]
    advance(w0, into(v0), kzl, kl, 2, 5, True)
    advance(w0, into(v0), kz, k, 5, 6, True, 4)
    for h in range(2):
        v0[6, h] = a[2, h]
        v0[7, h] = a[3, h]
    advance(v0, into(w0), kzl, kl, 3, 5, True)
    advance(v0, into(w0), kz, k, 5, 7, True, 4)
    for h in range(2):
        w0[7, h] = b[3, h]
        w0[8, h] = b[4, h]
    advance(w0, into_fine(fine, 4), kzl, kl, 4, 5, True)
    advance(w0, into_fine(fine, 4), kz, k, 5, 8, True, 4)
    out[0] = pooled(block_sums(fine, 0, 0), pool[...]) - stepped[0]


def weights_kernel(at, cc, kz, k):
    masks = coarse_masks()
    faces = [(cc[i] + cc[i + 1]) * (0.5 * COARSE_RATE) for i in range(7)]
    faces[2] = jnp.where(at[1] > 0, faces[2], 0.0)
    faces[6] = jnp.where(at[2] > 0, faces[6], 0.0)
    for i in range(7):
        kz[i] = faces[i]
    for i in range(6):
        for f, a in enumerate(coarse_weights(cc[i + 1], faces[i] + faces[i + 1], masks)):
            k[i, f] = a


def final_kernel(at, near, far, other, own_start, kz, k, spread, tall, lower, upper, out, made, sems):
    par, slice_at = at[0], at[3]

    def pick(level, p):
        return jnp.where((par == 1) == (level == 1), near[p + 2], other[5 - p])

    def gate(level, a):
        return jnp.where(slice_at >= level, a, 0.0)

    def grow(d, lo, hi):
        return {
            p: coarse_step(d[p], d[p + 1], d[p - 1], kz[p + 3], kz[p + 2], [k[p + 2, i] for i in range(5)])
            for p in range(lo, hi)
        }

    d = {p: gate(3, jnp.where(par == 1, far[p + 3], other[14 - p])) for p in range(-3, 5)}
    u = grow(d, -2, 4)
    d = {p: u[p] + gate(2, pick(2, p)) for p in range(-2, 4)}
    u = grow(d, -1, 3)
    d = {p: gate(1, u[p] + pick(1, p) - own_start[p + 1]) for p in range(-1, 3)}
    u = grow(d, 0, 2)
    wide = split_dot(jnp.concatenate([u[0], u[1]], axis=0), spread[...])
    high = wide.astype(BF16)
    low = (wide - high.astype(F32)).astype(BF16)
    change = mxu(tall[...], high) + mxu(tall[...], low)
    copies = []
    for half, fine in ((0, lower), (1, upper)):

        @pl.loop(0, 4)
        def _(i):
            for side in range(2):
                for h in range(2):
                    rows = slice(32 * side, 32 * side + 32)
                    cut = change[32 * half : 32 * half + 32, 256 * side + LANES * h : 256 * side + LANES * (h + 1)]
                    made[half, fast_plane(par, i), rows, LANES * h : LANES * (h + 1)] = fine[i, h, rows] + cut

        first = HALF * (par if half == 0 else 1 - par)
        copies.append(pltpu.make_async_copy(made.at[half], out.at[pl.ds(first, HALF)], sems.at[half]))
        copies[-1].start()
    for copy in copies:
        copy.wait()


def call(kernel, outs, scratch, flops, count):
    return pl.pallas_call(
        kernel,
        out_shape=[jax.ShapeDtypeStruct(s, F32) for s in outs],
        in_specs=[pl.BlockSpec(memory_space=pltpu.SMEM)]
        + [pl.BlockSpec(memory_space=pltpu.VMEM)] * (count - 1),
        out_specs=[pl.BlockSpec(memory_space=pltpu.VMEM)] * len(outs),
        scratch_shapes=[pltpu.VMEM(s, F32) for s in scratch],
        compiler_params=pltpu.CompilerParams(vmem_limit_bytes=VMEM_LIMIT),
        cost_estimate=pl.CostEstimate(flops=flops, bytes_accessed=flops // 4, transcendentals=0),
    )


def per_device(states, conductivity):
    return iteration(states[0], conductivity)[None]


def iteration(v, c):
    planes, rows, cols = v.shape
    plane = (rows, cols)
    wide, padded, block = (2, ROWS, LANES), (2, PADDED, LANES), (8, LANES)
    k, n = lax.axis_index("space"), lax.axis_index("tm")
    count, slices = lax.axis_size("space"), lax.axis_size("tm")
    par = k % 2
    mate = k + 1 - 2 * par
    inside = lambda i: ((i != 0) & (i != count - 1)).astype(jnp.int32)
    at = jnp.stack([par, inside(k), inside(mate), n]).astype(jnp.int32)

    slow_pairs = [(i, i + 1) for i in range(1, count - 1, 2)]
    slow_pairs += [(b, a) for a, b in slow_pairs]
    fast_pairs = [(i, i ^ 1) for i in range(count)]
    slow = lambda x: lax.ppermute(x, "space", slow_pairs)
    fast = lambda x: lax.ppermute(x, "space", fast_pairs)

    half = (2 * HALF,) + plane
    near_slow, near_fast, pool, spread, tall = pl.pallas_call(
        pack_kernel,
        out_shape=[jax.ShapeDtypeStruct(half, F32)] * 2
        + [jax.ShapeDtypeStruct(m, BF16) for m in ((512, LANES), (LANES, 512), (64, 16))],
        in_specs=[pl.BlockSpec(memory_space=pltpu.SMEM)] + [pl.BlockSpec(memory_space=pltpu.HBM)] * 2,
        out_specs=[pl.BlockSpec(memory_space=pltpu.VMEM)] * 5,
        scratch_shapes=[pltpu.SemaphoreType.DMA((4,))],
        compiler_params=pltpu.CompilerParams(vmem_limit_bytes=VMEM_LIMIT),
    )(at, *(pltpu.with_memory_space_constraint(x, pltpu.HBM) for x in (v, c)))
    from_slow = slow(near_slow)
    from_fast = fast(near_fast)

    (own,) = call(coarse_kernel, [(4,) + block], [(8,) + padded] * 2, 1_000_000, 4)(at, near_slow, near_fast, pool)
    theirs = fast(own)
    a, b, kz, kk, upper, end = call(
        early_kernel,
        [(12,) + padded, (12,) + padded, (11,) + wide, (11, 5) + wide, (4,) + wide, (1,) + block],
        [(12,) + padded],
        8_000_000,
        5,
    )(at, near_slow, near_fast, from_fast, pool)
    mate_end = fast(end)
    lower, first, before = call(
        late_kernel,
        [(4,) + wide, (6,) + block, (1,) + block],
        [(10,) + padded] * 3 + [(5, 5) + wide, (5,) + wide],
        4_000_000,
        12,
    )(at, near_slow, from_slow, a, b, kz, kk, pool, own, theirs, end, mate_end)
    beyond = slow(first)
    late = fast(jnp.concatenate([first[:1], beyond[:4]]))

    line = jnp.stack(
        [beyond[2], beyond[1], beyond[0], first[0], first[1], first[2], late[0], late[1], late[2], late[3]]
    )
    pairs = []
    for i in range(count):
        step = 2 - i % 2
        pairs += [(s * count + i, (s + step) * count + i) for s in range(slices - step)]
    near = lax.ppermute(line[1:9], ("tm", "space"), pairs)
    far = lax.ppermute(line, ("tm", "space"), [(i, (slices - 1) * count + i) for i in range(1, count, 2)])
    cc = jnp.stack([beyond[5], beyond[4], beyond[3], own[2], own[3], theirs[3], theirs[2], late[4]])
    ckz, ck = call(weights_kernel, [(7,) + block, (6, 5) + block], [], 100_000, 2)(at, cc)
    own_start = jnp.concatenate([before, own[:2], theirs[1:2]])
    other = fast(jnp.concatenate([near, far]))
    return pl.pallas_call(
        final_kernel,
        out_shape=jax.ShapeDtypeStruct((planes,) + plane, F32),
        in_specs=[pl.BlockSpec(memory_space=pltpu.SMEM)] + [pl.BlockSpec(memory_space=pltpu.VMEM)] * 10,
        out_specs=pl.BlockSpec(memory_space=pl.ANY),
        scratch_shapes=[pltpu.VMEM((2, HALF) + plane, F32), pltpu.SemaphoreType.DMA((2,))],
        compiler_params=pltpu.CompilerParams(vmem_limit_bytes=VMEM_LIMIT),
    )(at, near, far, other, own_start, ckz, ck, spread, tall, lower, upper)


def solution(mesh):
    return jax.shard_map(
        per_device,
        mesh=mesh,
        in_specs=(P("tm", "space", None, None), P("space", None, None)),
        out_specs=P("tm", "space", None, None),
        check_vma=False,
    )
```

```python
import jax
import jax.numpy as jnp
from jax import lax
from jax.experimental import pallas as pl
from jax.experimental.pallas import tpu as pltpu
from jax.sharding import PartitionSpec as P


FSTEPS = 4
COARSEN = 4
FINE_RATE = 0.1
COARSE_RATE = FINE_RATE * FSTEPS / 16.0
HALF = 4
F32 = jnp.float32
BF16 = jnp.bfloat16
VMEM_LIMIT = 24 * 1024 * 1024
LANES = 128
ROWS = 64
TOP = 8
PADDED = 80
UNROLL = True
CHUNK = 8


def place():
    k, count = lax.axis_index("space"), lax.axis_size("space")
    inside = lambda i: (i != 0) & (i != count - 1)
    par = k % 2
    return par, inside(k), inside(k + 1 - 2 * par), lax.axis_index("tm")


def fast_plane(par, i):
    return i + par * (3 - 2 * i)


def slow_plane(par, i):
    return (3 - i) + par * (2 * i - 3)


def rows_of(ref, p, h, shift=0):
    return ref[p, h, TOP + shift : TOP + ROWS + shift, :]


def put(ref, p, plane):
    for h in range(2):
        ref[p, h, TOP : TOP + ROWS, :] = plane[:, h * LANES : (h + 1) * LANES]


def blank_margins(ref, planes):
    for p in range(planes):
        for h in range(2):
            ref[p, h, 0:TOP, :] = jnp.zeros((TOP, LANES), F32)
            ref[p, h, TOP + ROWS : PADDED, :] = jnp.zeros((TOP, LANES), F32)


def mirror_margins(ref, p):
    for h in range(2):
        ref[p, h, TOP - 1 : TOP, :] = -ref[p, h, TOP : TOP + 1, :]
        ref[p, h, TOP + ROWS : TOP + ROWS + 1, :] = -ref[p, h, TOP + ROWS - 1 : TOP + ROWS, :]


def lane_turns(a0, a1):
    at = lax.broadcasted_iota(jnp.int32, a0.shape, 1)
    up0, up1 = pltpu.roll(a0, LANES - 1, 1), pltpu.roll(a1, LANES - 1, 1)
    down0, down1 = pltpu.roll(a0, 1, 1), pltpu.roll(a1, 1, 1)
    return (jnp.where(at == LANES - 1, up1, up0), up1), (down0, jnp.where(at == 0, down0, down1)), at


def fill_faces(c, kz, lo, hi, scale, unroll):
    @pl.loop(lo, hi, unroll=unroll)
    def _(p):
        for h in range(2):
            kz[p, h] = (rows_of(c, p, h) + rows_of(c, p + 1, h)) * scale


def fill_coefficients(c, kz, k, lo, hi, scale, unroll):
    @pl.loop(lo, hi, unroll=unroll)
    def _(p):
        a0, a1 = rows_of(c, p, 0), rows_of(c, p, 1)
        (up0, up1), (down0, down1), at = lane_turns(a0, a1)
        up1 = jnp.where(at == LANES - 1, -a1, up1)
        down0 = jnp.where(at == 0, -a0, down0)
        for h, a, up, down in ((0, a0, up0, down0), (1, a1, up1, down1)):
            kxu = (a + rows_of(c, p, h, 1)) * scale
            kxd = (a + rows_of(c, p, h, -1)) * scale
            kyu = (a + up) * scale
            kyd = (a + down) * scale
            k[p, 0, h] = 1.0 - ((kxu + kxd) + (kyu + kyd) + (kz[p, h] + kz[p - 1, h]))
            k[p, 1, h] = kxu
            k[p, 2, h] = kxd
            k[p, 3, h] = kyu
            k[p, 4, h] = kyd


def advance(src, store, kz, k, lo, hi, unroll, shift=0):
    at = lax.broadcasted_iota(jnp.int32, (CHUNK, LANES), 1)

    def some(p):
        q = p - shift
        made = []
        for r in range(0, ROWS, CHUNK):
            cut = lambda ref, i, h, s=0: ref[i, h, TOP + r + s : TOP + r + s + CHUNK, :]
            w = lambda i, h: k[q, i, h, r : r + CHUNK, :]
            v = [cut(src, p, h) for h in range(2)]
            up = [pltpu.roll(v[h], LANES - 1, 1) for h in range(2)]
            down = [pltpu.roll(v[h], 1, 1) for h in range(2)]
            up = [jnp.where(at == LANES - 1, up[1], up[0]), up[1]]
            down = [down[0], jnp.where(at == 0, down[0], down[1])]
            for h in range(2):
                a = w(0, h) * v[h]
                b = kz[q, h, r : r + CHUNK] * cut(src, p + 1, h) + kz[q - 1, h, r : r + CHUNK] * cut(src, p - 1, h)
                d = w(1, h) * cut(src, p, h, 1) + w(2, h) * cut(src, p, h, -1)
                e = w(3, h) * up[h] + w(4, h) * down[h]
                made.append((r, h, (a + b) + (d + e)))
        return made

    @pl.loop(lo, hi, unroll=unroll)
    def _(p):
        for r, h, a in some(p):
            store(p, h, r, a)


def into(ref):
    def store(p, h, r, a):
        ref[p, h, TOP + r : TOP + r + CHUNK, :] = a

    return store


def into_fine(ref, shift):
    def store(p, h, r, a):
        ref[p - shift, h, r : r + CHUNK, :] = a

    return store


def block_sums(ref, first, top):
    parts = []
    for side in range(2):
        for h in range(2):
            total = None
            for p in range(first, first + COARSEN):
                for r in range(COARSEN):
                    term = ref[p, h, pl.ds(top + 32 * side + r, 8, stride=COARSEN), :]
                    total = term if total is None else total + term
            parts.append(total)
    return jnp.concatenate(parts, axis=1)


def mxu(a, b):
    return lax.dot_general(a, b, (((1,), (0,)), ((), ())), preferred_element_type=F32)


def split_dot(a, b):
    high = a.astype(BF16)
    low = (a - high.astype(F32)).astype(BF16)
    return mxu(high, b) + mxu(low, b)


def pooled(sums, pool):
    return split_dot(sums, pool) * (1.0 / COARSEN**3)


def matches(rows, cols, by_row):
    r = lax.broadcasted_iota(jnp.int32, (rows, cols), 0)
    c = lax.broadcasted_iota(jnp.int32, (rows, cols), 1)
    same = r // COARSEN == c if by_row else c // COARSEN == r
    return jnp.where(same, 1.0, 0.0).astype(BF16)


def pack_kernel(v, c, near_slow, near_fast, pool, spread, tall, sems):
    par = place()[0]
    copies = []
    for s, (ref, side) in enumerate(((near_slow, par), (near_fast, 1 - par))):
        for f, src in enumerate((v, c)):
            copies.append(
                pltpu.make_async_copy(
                    src.at[pl.ds(side * HALF, HALF)], ref.at[pl.ds(f * HALF, HALF)], sems.at[2 * s + f]
                )
            )
    for copy in copies:
        copy.start()
    pool[...] = matches(*pool.shape, True)
    spread[...] = matches(*spread.shape, False)
    tall[...] = matches(*tall.shape, True)
    for copy in copies:
        copy.wait()


def put_own(par, near_slow, near_fast, field, coefficient):
    @pl.loop(0, 4)
    def _(i):
        for base, ref in ((0, near_slow), (4, near_fast)):
            put(field, base + i, ref[fast_plane(par, i)])
            put(coefficient, base + i, ref[HALF + fast_plane(par, i)])


def coarse_kernel(near_slow, near_fast, pool, out, v0, c0):
    put_own(place()[0], near_slow, near_fast, v0, c0)
    sums = [block_sums(ref, 4 * b, TOP) for ref in (v0, c0) for b in range(2)]
    res = pooled(jnp.concatenate(sums, axis=0), pool[...])
    for i in range(4):
        out[i] = res[8 * i : 8 * i + 8]


def early_kernel(near_slow, near_fast, h, pool, a, b, kz, k, fine, end, c0):
    par = place()[0]
    blank_margins(a, 12)
    blank_margins(b, 12)
    put_own(par, near_slow, near_fast, a, c0)

    @pl.loop(0, 4)
    def _(i):
        put(a, 8 + i, h[fast_plane(par, i)])
        put(c0, 8 + i, h[HALF + fast_plane(par, i)])

    for i in range(12):
        mirror_margins(c0, i)
    scale = 0.5 * FINE_RATE
    fill_faces(c0, kz, 0, 11, scale, UNROLL)
    fill_coefficients(c0, kz, k, 1, 11, scale, UNROLL)
    advance(a, into(b), kz, k, 1, 11, UNROLL)
    advance(b, into(a), kz, k, 2, 10, UNROLL)
    advance(a, into(b), kz, k, 3, 9, UNROLL)
    advance(b, into_fine(fine, 4), kz, k, 4, 8, UNROLL)
    end[0] = pooled(block_sums(fine, 0, 0), pool[...])


def row_turns(a):
    other = pltpu.roll(a, LANES // 2, 1)
    row = lax.broadcasted_iota(jnp.int32, a.shape, 0)
    up = jnp.where(row == 7, pltpu.roll(other, 7, 0), pltpu.roll(a, 7, 0))
    down = jnp.where(row == 0, pltpu.roll(other, 1, 0), pltpu.roll(a, 1, 0))
    return up, down


def coarse_masks():
    scale = 0.5 * COARSE_RATE
    row = lax.broadcasted_iota(jnp.int32, (8, LANES), 0)
    lane = lax.broadcasted_iota(jnp.int32, (8, LANES), 1)
    left = lane < LANES // 2
    up = jnp.where(left | (row < 7), scale, 0.0)
    down = jnp.where(left & (row == 0), 0.0, scale)
    right = jnp.where(lane % (LANES // 2) == LANES // 2 - 1, 0.0, scale)
    before = jnp.where(lane % (LANES // 2) == 0, 0.0, scale)
    return up, down, right, before


def coarse_weights(c, faces, masks):
    up, down = row_turns(c)
    kxu, kxd = (c + up) * masks[0], (c + down) * masks[1]
    kyu = (c + pltpu.roll(c, LANES - 1, 1)) * masks[2]
    kyd = (c + pltpu.roll(c, 1, 1)) * masks[3]
    return 1.0 - ((kxu + kxd) + (kyu + kyd) + faces), kxu, kxd, kyu, kyd


def coarse_step(v, above, below, face_above, face_below, w):
    up, down = row_turns(v)
    x = w[1] * up + w[2] * down
    y = w[3] * pltpu.roll(v, LANES - 1, 1) + w[4] * pltpu.roll(v, 1, 1)
    return (w[0] * v + (face_above * above + face_below * below)) + (x + y)


def late_kernel(
    near_slow, g, a, b, kz, k, pool, own, theirs, end, mate_end, fine, out, before, v0, c0, w0, kl, kzl
):
    par = place()[0]
    blank_margins(v0, 10)
    blank_margins(w0, 10)

    @pl.loop(0, 4)
    def _(i):
        put(v0, 3 - i, g[slow_plane(par, i)])
        put(c0, 3 - i, g[HALF + slow_plane(par, i)])

    for i in range(2):
        put(v0, 4 + i, near_slow[fast_plane(par, i)])
        put(c0, 4 + i, near_slow[HALF + fast_plane(par, i)])
    for i in range(6):
        mirror_margins(c0, i)
    beyond = pooled(jnp.concatenate([block_sums(v0, 0, TOP), block_sums(c0, 0, TOP)], axis=0), pool[...])
    start = [beyond[:8], own[0], own[1], theirs[1], theirs[0]]
    cc = [beyond[8:], own[2], own[3], theirs[3], theirs[2]]
    faces = [(cc[i] + cc[i + 1]) * (0.5 * COARSE_RATE) for i in range(4)]
    faces[0] = jnp.where(place()[1], faces[0], 0.0)
    masks = coarse_masks()
    before[0] = start[0]
    stepped = []
    for i in range(1, 4):
        w = coarse_weights(cc[i], faces[i] + faces[i - 1], masks)
        step = coarse_step(start[i], start[i + 1], start[i - 1], faces[i], faces[i - 1], w)
        stepped.append(jnp.where(place()[3] > 0, step, 0.0))
        out[2 + i] = cc[i]
    out[1] = end[0] - stepped[1]
    out[2] = mate_end[0] - stepped[2]
    scale = 0.5 * FINE_RATE
    fill_faces(c0, kzl, 0, 5, scale, True)
    for h in range(2):
        kzl[3, h] = jnp.where(place()[1], kzl[3, h], 0.0)
    fill_coefficients(c0, kzl, kl, 1, 5, scale, True)
    advance(v0, into(w0), kzl, kl, 1, 5, True)
    for h in range(2):
        w0[5, h] = b[1, h]
        w0[6, h] = b[2, h]
    advance(w0, into(v0), kzl, kl, 2, 5, True)
    advance(w0, into(v0), kz, k, 5, 6, True, 4)
    for h in range(2):
        v0[6, h] = a[2, h]
        v0[7, h] = a[3, h]
    advance(v0, into(w0), kzl, kl, 3, 5, True)
    advance(v0, into(w0), kz, k, 5, 7, True, 4)
    for h in range(2):
        w0[7, h] = b[3, h]
        w0[8, h] = b[4, h]
    advance(w0, into_fine(fine, 4), kzl, kl, 4, 5, True)
    advance(w0, into_fine(fine, 4), kz, k, 5, 8, True, 4)
    out[0] = pooled(block_sums(fine, 0, 0), pool[...]) - stepped[0]


def weights_kernel(cc, kz, k):
    masks = coarse_masks()
    faces = [(cc[i] + cc[i + 1]) * (0.5 * COARSE_RATE) for i in range(7)]
    faces[2] = jnp.where(place()[1], faces[2], 0.0)
    faces[6] = jnp.where(place()[2], faces[6], 0.0)
    for i in range(7):
        kz[i] = faces[i]
    for i in range(6):
        for f, a in enumerate(coarse_weights(cc[i + 1], faces[i] + faces[i + 1], masks)):
            k[i, f] = a


def final_kernel(near, far, other, own_start, kz, k, spread, tall, lower, upper, out, made, sems):
    par, _, _, slice_at = place()

    def pick(level, p):
        return jnp.where((par == 1) == (level == 1), near[p + 2], other[5 - p])

    def gate(level, a):
        return jnp.where(slice_at >= level, a, 0.0)

    def grow(d, lo, hi):
        return {
            p: coarse_step(d[p], d[p + 1], d[p - 1], kz[p + 3], kz[p + 2], [k[p + 2, i] for i in range(5)])
            for p in range(lo, hi)
        }

    d = {p: gate(3, jnp.where(par == 1, far[p + 3], other[14 - p])) for p in range(-3, 5)}
    u = grow(d, -2, 4)
    d = {p: u[p] + gate(2, pick(2, p)) for p in range(-2, 4)}
    u = grow(d, -1, 3)
    d = {p: gate(1, u[p] + pick(1, p) - own_start[p + 1]) for p in range(-1, 3)}
    u = grow(d, 0, 2)
    wide = split_dot(jnp.concatenate([u[0], u[1]], axis=0), spread[...])
    high = wide.astype(BF16)
    low = (wide - high.astype(F32)).astype(BF16)
    change = mxu(tall[...], high) + mxu(tall[...], low)
    copies = []
    for half, fine in ((0, lower), (1, upper)):

        @pl.loop(0, 4)
        def _(i):
            for side in range(2):
                for h in range(2):
                    rows = slice(32 * side, 32 * side + 32)
                    cut = change[32 * half : 32 * half + 32, 256 * side + LANES * h : 256 * side + LANES * (h + 1)]
                    made[half, fast_plane(par, i), rows, LANES * h : LANES * (h + 1)] = fine[i, h, rows] + cut

        first = HALF * (par if half == 0 else 1 - par)
        copies.append(pltpu.make_async_copy(made.at[half], out.at[pl.ds(first, HALF)], sems.at[half]))
        copies[-1].start()
    for copy in copies:
        copy.wait()


def call(kernel, outs, scratch, flops, count):
    return pl.pallas_call(
        kernel,
        out_shape=[jax.ShapeDtypeStruct(s, F32) for s in outs],
        in_specs=[pl.BlockSpec(memory_space=pltpu.VMEM)] * count,
        out_specs=[pl.BlockSpec(memory_space=pltpu.VMEM)] * len(outs),
        scratch_shapes=[pltpu.VMEM(s, F32) for s in scratch],
        compiler_params=pltpu.CompilerParams(vmem_limit_bytes=VMEM_LIMIT),
        cost_estimate=pl.CostEstimate(flops=flops, bytes_accessed=flops // 4, transcendentals=0),
    )


def per_device(states, conductivity):
    return iteration(states[0], conductivity)[None]


def iteration(v, c):
    planes, rows, cols = v.shape
    plane = (rows, cols)
    wide, padded, block = (2, ROWS, LANES), (2, PADDED, LANES), (8, LANES)
    count, slices = lax.axis_size("space"), lax.axis_size("tm")

    slow_pairs = [(i, i + 1) for i in range(1, count - 1, 2)]
    slow_pairs += [(b, a) for a, b in slow_pairs]
    fast_pairs = [(i, i ^ 1) for i in range(count)]
    slow = lambda x: lax.ppermute(x, "space", slow_pairs)
    fast = lambda x: lax.ppermute(x, "space", fast_pairs)

    half = (2 * HALF,) + plane
    near_slow, near_fast, pool, spread, tall = pl.pallas_call(
        pack_kernel,
        out_shape=[jax.ShapeDtypeStruct(half, F32)] * 2
        + [jax.ShapeDtypeStruct(m, BF16) for m in ((512, LANES), (LANES, 512), (64, 16))],
        in_specs=[pl.BlockSpec(memory_space=pltpu.HBM)] * 2,
        out_specs=[pl.BlockSpec(memory_space=pltpu.VMEM)] * 5,
        scratch_shapes=[pltpu.SemaphoreType.DMA((4,))],
        compiler_params=pltpu.CompilerParams(vmem_limit_bytes=VMEM_LIMIT),
    )(*(pltpu.with_memory_space_constraint(x, pltpu.HBM) for x in (v, c)))
    from_slow = slow(near_slow)
    from_fast = fast(near_fast)

    (own,) = call(coarse_kernel, [(4,) + block], [(8,) + padded] * 2, 1_000_000, 3)(near_slow, near_fast, pool)
    theirs = fast(own)
    a, b, kz, kk, upper, end = call(
        early_kernel,
        [(12,) + padded, (12,) + padded, (11,) + wide, (11, 5) + wide, (4,) + wide, (1,) + block],
        [(12,) + padded],
        8_000_000,
        4,
    )(near_slow, near_fast, from_fast, pool)
    mate_end = fast(end)
    lower, first, before = call(
        late_kernel,
        [(4,) + wide, (6,) + block, (1,) + block],
        [(10,) + padded] * 3 + [(5, 5) + wide, (5,) + wide],
        4_000_000,
        11,
    )(near_slow, from_slow, a, b, kz, kk, pool, own, theirs, end, mate_end)
    beyond = slow(first)
    late = fast(jnp.concatenate([first[:1], beyond[:4]]))

    line = jnp.stack(
        [beyond[2], beyond[1], beyond[0], first[0], first[1], first[2], late[0], late[1], late[2], late[3]]
    )
    pairs = []
    for i in range(count):
        step = 2 - i % 2
        pairs += [(s * count + i, (s + step) * count + i) for s in range(slices - step)]
    near = lax.ppermute(line[1:9], ("tm", "space"), pairs)
    far = lax.ppermute(line, ("tm", "space"), [(i, (slices - 1) * count + i) for i in range(1, count, 2)])
    cc = jnp.stack([beyond[5], beyond[4], beyond[3], own[2], own[3], theirs[3], theirs[2], late[4]])
    ckz, ck = call(weights_kernel, [(7,) + block, (6, 5) + block], [], 100_000, 1)(cc)
    own_start = jnp.concatenate([before, own[:2], theirs[1:2]])
    other = fast(jnp.concatenate([near, far]))
    return pl.pallas_call(
        final_kernel,
        out_shape=jax.ShapeDtypeStruct((planes,) + plane, F32),
        in_specs=[pl.BlockSpec(memory_space=pltpu.VMEM)] * 10,
        out_specs=pl.BlockSpec(memory_space=pl.ANY),
        scratch_shapes=[pltpu.VMEM((2, HALF) + plane, F32), pltpu.SemaphoreType.DMA((2,))],
        compiler_params=pltpu.CompilerParams(vmem_limit_bytes=VMEM_LIMIT),
    )(near, far, other, own_start, ckz, ck, spread, tall, lower, upper)


def solution(mesh):
    return jax.shard_map(
        per_device,
        mesh=mesh,
        in_specs=(P("tm", "space", None, None), P("space", None, None)),
        out_specs=P("tm", "space", None, None),
        check_vma=False,
    )
```

```python
import jax
import jax.numpy as jnp
from jax import lax
from jax.experimental import pallas as pl
from jax.experimental.pallas import tpu as pltpu
from jax.sharding import PartitionSpec as P


FSTEPS = 4
COARSEN = 4
FINE_RATE = 0.1
COARSE_RATE = FINE_RATE * FSTEPS / 16.0
HALF = 4
F32 = jnp.float32
BF16 = jnp.bfloat16
VMEM_LIMIT = 24 * 1024 * 1024
LANES = 128
ROWS = 64
TOP = 8
PADDED = 80
UNROLL = True
CHUNK = 8


def place():
    k, count = lax.axis_index("space"), lax.axis_size("space")
    inside = lambda i: (i != 0) & (i != count - 1)
    par = k % 2
    return par, inside(k), inside(k + 1 - 2 * par), lax.axis_index("tm")


def own_plane(par, i):
    return i + par * (7 - 2 * i)


def half_plane(par, i):
    return i + par * (3 - 2 * i)


def slow_plane(par, i):
    return (7 - i) + par * (2 * i - 7)


def rows_of(ref, p, h, shift=0):
    return ref[p, h, TOP + shift : TOP + ROWS + shift, :]


def put(ref, p, plane):
    for h in range(2):
        ref[p, h, TOP : TOP + ROWS, :] = plane[:, h * LANES : (h + 1) * LANES]


def blank_margins(ref, planes):
    for p in range(planes):
        for h in range(2):
            ref[p, h, 0:TOP, :] = jnp.zeros((TOP, LANES), F32)
            ref[p, h, TOP + ROWS : PADDED, :] = jnp.zeros((TOP, LANES), F32)


def mirror_margins(ref, p):
    for h in range(2):
        ref[p, h, TOP - 1 : TOP, :] = -ref[p, h, TOP : TOP + 1, :]
        ref[p, h, TOP + ROWS : TOP + ROWS + 1, :] = -ref[p, h, TOP + ROWS - 1 : TOP + ROWS, :]


def lane_turns(a0, a1):
    at = lax.broadcasted_iota(jnp.int32, a0.shape, 1)
    up0, up1 = pltpu.roll(a0, LANES - 1, 1), pltpu.roll(a1, LANES - 1, 1)
    down0, down1 = pltpu.roll(a0, 1, 1), pltpu.roll(a1, 1, 1)
    return (jnp.where(at == LANES - 1, up1, up0), up1), (down0, jnp.where(at == 0, down0, down1)), at


def fill_faces(c, kz, lo, hi, scale, unroll):
    @pl.loop(lo, hi, unroll=unroll)
    def _(p):
        for h in range(2):
            kz[p, h] = (rows_of(c, p, h) + rows_of(c, p + 1, h)) * scale


def fill_coefficients(c, kz, k, lo, hi, scale, unroll):
    @pl.loop(lo, hi, unroll=unroll)
    def _(p):
        a0, a1 = rows_of(c, p, 0), rows_of(c, p, 1)
        (up0, up1), (down0, down1), at = lane_turns(a0, a1)
        up1 = jnp.where(at == LANES - 1, -a1, up1)
        down0 = jnp.where(at == 0, -a0, down0)
        for h, a, up, down in ((0, a0, up0, down0), (1, a1, up1, down1)):
            kxu = (a + rows_of(c, p, h, 1)) * scale
            kxd = (a + rows_of(c, p, h, -1)) * scale
            kyu = (a + up) * scale
            kyd = (a + down) * scale
            k[p, 0, h] = 1.0 - ((kxu + kxd) + (kyu + kyd) + (kz[p, h] + kz[p - 1, h]))
            k[p, 1, h] = kxu
            k[p, 2, h] = kxd
            k[p, 3, h] = kyu
            k[p, 4, h] = kyd


def advance(src, store, kz, k, lo, hi, unroll, shift=0):
    at = lax.broadcasted_iota(jnp.int32, (CHUNK, LANES), 1)

    def some(p):
        q = p - shift
        made = []
        for r in range(0, ROWS, CHUNK):
            cut = lambda ref, i, h, s=0: ref[i, h, TOP + r + s : TOP + r + s + CHUNK, :]
            w = lambda i, h: k[q, i, h, r : r + CHUNK, :]
            v = [cut(src, p, h) for h in range(2)]
            up = [pltpu.roll(v[h], LANES - 1, 1) for h in range(2)]
            down = [pltpu.roll(v[h], 1, 1) for h in range(2)]
            up = [jnp.where(at == LANES - 1, up[1], up[0]), up[1]]
            down = [down[0], jnp.where(at == 0, down[0], down[1])]
            for h in range(2):
                a = w(0, h) * v[h]
                b = kz[q, h, r : r + CHUNK] * cut(src, p + 1, h) + kz[q - 1, h, r : r + CHUNK] * cut(src, p - 1, h)
                d = w(1, h) * cut(src, p, h, 1) + w(2, h) * cut(src, p, h, -1)
                e = w(3, h) * up[h] + w(4, h) * down[h]
                made.append((r, h, (a + b) + (d + e)))
        return made

    @pl.loop(lo, hi, unroll=unroll)
    def _(p):
        for r, h, a in some(p):
            store(p, h, r, a)


def into(ref):
    def store(p, h, r, a):
        ref[p, h, TOP + r : TOP + r + CHUNK, :] = a

    return store


def into_fine(ref, shift):
    def store(p, h, r, a):
        ref[p - shift, h, r : r + CHUNK, :] = a

    return store


def block_sums(ref, first, top):
    parts = []
    for side in range(2):
        for h in range(2):
            total = None
            for p in range(first, first + COARSEN):
                for r in range(COARSEN):
                    term = ref[p, h, pl.ds(top + 32 * side + r, 8, stride=COARSEN), :]
                    total = term if total is None else total + term
            parts.append(total)
    return jnp.concatenate(parts, axis=1)


def mxu(a, b):
    return lax.dot_general(a, b, (((1,), (0,)), ((), ())), preferred_element_type=F32)


def split_dot(a, b):
    high = a.astype(BF16)
    low = (a - high.astype(F32)).astype(BF16)
    return mxu(high, b) + mxu(low, b)


def pooled(sums, pool):
    return split_dot(sums, pool) * (1.0 / COARSEN**3)


def matches(rows, cols, by_row):
    r = lax.broadcasted_iota(jnp.int32, (rows, cols), 0)
    c = lax.broadcasted_iota(jnp.int32, (rows, cols), 1)
    same = r // COARSEN == c if by_row else c // COARSEN == r
    return jnp.where(same, 1.0, 0.0).astype(BF16)


def pack_kernel(v, c, whole, pool, spread, tall, sems):
    copies = [
        pltpu.make_async_copy(src, whole.at[pl.ds(f * 8, 8)], sems.at[f]) for f, src in enumerate((v, c))
    ]
    for copy in copies:
        copy.start()
    pool[...] = matches(*pool.shape, True)
    spread[...] = matches(*spread.shape, False)
    tall[...] = matches(*tall.shape, True)
    for copy in copies:
        copy.wait()


def put_own(par, whole, field, coefficient):
    @pl.loop(0, 8)
    def _(i):
        put(field, i, whole[own_plane(par, i)])
        put(coefficient, i, whole[8 + own_plane(par, i)])


def coarse_kernel(whole, pool, out, v0, c0):
    put_own(place()[0], whole, v0, c0)
    sums = [block_sums(ref, 4 * b, TOP) for ref in (v0, c0) for b in range(2)]
    res = pooled(jnp.concatenate(sums, axis=0), pool[...])
    for i in range(4):
        out[i] = res[8 * i : 8 * i + 8]


def early_kernel(whole, h, pool, a, b, kz, k, fine, end, c0):
    par = place()[0]
    blank_margins(a, 12)
    blank_margins(b, 12)
    put_own(par, whole, a, c0)

    @pl.loop(0, 4)
    def _(i):
        put(a, 8 + i, h[own_plane(par, i)])
        put(c0, 8 + i, h[8 + own_plane(par, i)])

    for i in range(12):
        mirror_margins(c0, i)
    scale = 0.5 * FINE_RATE
    fill_faces(c0, kz, 0, 11, scale, UNROLL)
    fill_coefficients(c0, kz, k, 1, 11, scale, UNROLL)
    advance(a, into(b), kz, k, 1, 11, UNROLL)
    advance(b, into(a), kz, k, 2, 10, UNROLL)
    advance(a, into(b), kz, k, 3, 9, UNROLL)
    advance(b, into_fine(fine, 4), kz, k, 4, 8, UNROLL)
    end[0] = pooled(block_sums(fine, 0, 0), pool[...])


def row_turns(a):
    other = pltpu.roll(a, LANES // 2, 1)
    row = lax.broadcasted_iota(jnp.int32, a.shape, 0)
    up = jnp.where(row == 7, pltpu.roll(other, 7, 0), pltpu.roll(a, 7, 0))
    down = jnp.where(row == 0, pltpu.roll(other, 1, 0), pltpu.roll(a, 1, 0))
    return up, down


def coarse_masks():
    scale = 0.5 * COARSE_RATE
    row = lax.broadcasted_iota(jnp.int32, (8, LANES), 0)
    lane = lax.broadcasted_iota(jnp.int32, (8, LANES), 1)
    left = lane < LANES // 2
    up = jnp.where(left | (row < 7), scale, 0.0)
    down = jnp.where(left & (row == 0), 0.0, scale)
    right = jnp.where(lane % (LANES // 2) == LANES // 2 - 1, 0.0, scale)
    before = jnp.where(lane % (LANES // 2) == 0, 0.0, scale)
    return up, down, right, before


def coarse_weights(c, faces, masks):
    up, down = row_turns(c)
    kxu, kxd = (c + up) * masks[0], (c + down) * masks[1]
    kyu = (c + pltpu.roll(c, LANES - 1, 1)) * masks[2]
    kyd = (c + pltpu.roll(c, 1, 1)) * masks[3]
    return 1.0 - ((kxu + kxd) + (kyu + kyd) + faces), kxu, kxd, kyu, kyd


def coarse_step(v, above, below, face_above, face_below, w):
    up, down = row_turns(v)
    x = w[1] * up + w[2] * down
    y = w[3] * pltpu.roll(v, LANES - 1, 1) + w[4] * pltpu.roll(v, 1, 1)
    return (w[0] * v + (face_above * above + face_below * below)) + (x + y)


def coarse_change(start, cc, faces, i, masks):
    w = coarse_weights(cc[i], faces[i] + faces[i - 1], masks)
    step = coarse_step(start[i], start[i + 1], start[i - 1], faces[i], faces[i - 1], w)
    return jnp.where(place()[3] > 0, step, 0.0)


def jump_kernel(own, theirs, end, mate_end, out):
    start = [own[0], own[1], theirs[1], theirs[0]]
    cc = [own[2], own[3], theirs[3], theirs[2]]
    faces = [(cc[i] + cc[i + 1]) * (0.5 * COARSE_RATE) for i in range(3)]
    masks = coarse_masks()
    out[0] = end[0] - coarse_change(start, cc, faces, 1, masks)
    out[1] = mate_end[0] - coarse_change(start, cc, faces, 2, masks)
    for i in range(3):
        out[2 + i] = cc[i]


def late_kernel(whole, g, a, b, kz, k, pool, own, fine, out, before, v0, c0, w0, kl, kzl, extra):
    par, slow_ok, _, _ = place()
    blank_margins(v0, 14)
    blank_margins(w0, 14)

    @pl.loop(0, 8, unroll=True)
    def _(i):
        put(v0, 7 - i, g[slow_plane(par, i)])
        put(c0, 7 - i, g[8 + slow_plane(par, i)])

    for i in range(2):
        put(v0, 8 + i, whole[own_plane(par, i)])
        put(c0, 8 + i, whole[8 + own_plane(par, i)])
    for i in range(10):
        mirror_margins(c0, i)
    sums = [block_sums(ref, 4 * q, TOP) for ref in (v0, c0) for q in range(2)]
    beyond = pooled(jnp.concatenate(sums, axis=0), pool[...])
    start = [beyond[:8], beyond[8:16], own[0], own[1]]
    cc = [beyond[16:24], beyond[24:], own[2], own[3]]
    faces = [(cc[i] + cc[i + 1]) * (0.5 * COARSE_RATE) for i in range(3)]
    faces[1] = jnp.where(slow_ok, faces[1], 0.0)
    masks = coarse_masks()
    before[0] = start[1]
    stepped = [coarse_change(start, cc, faces, i, masks) for i in (1, 2)]
    scale = 0.5 * FINE_RATE
    fill_faces(c0, kzl, 0, 9, scale, True)
    for h in range(2):
        kzl[7, h] = jnp.where(slow_ok, kzl[7, h], 0.0)
    fill_coefficients(c0, kzl, kl, 1, 9, scale, True)
    advance(v0, into(w0), kzl, kl, 1, 9, True)
    for h in range(2):
        w0[9, h] = b[1, h]
        w0[10, h] = b[2, h]
    advance(w0, into(v0), kzl, kl, 2, 9, True)
    advance(w0, into(v0), kz, k, 9, 10, True, 8)
    for h in range(2):
        v0[10, h] = a[2, h]
        v0[11, h] = a[3, h]
    advance(v0, into(w0), kzl, kl, 3, 9, True)
    advance(v0, into(w0), kz, k, 9, 11, True, 8)
    for h in range(2):
        w0[11, h] = b[3, h]
        w0[12, h] = b[4, h]
    advance(w0, into_fine(extra, 4), kzl, kl, 4, 8, True)
    advance(w0, into_fine(fine, 8), kzl, kl, 8, 9, True)
    advance(w0, into_fine(fine, 8), kz, k, 9, 12, True, 8)
    ends = pooled(jnp.concatenate([block_sums(ref, 0, 0) for ref in (extra, fine)], axis=0), pool[...])
    out[0] = ends[8:] - stepped[1]
    out[1] = ends[:8] - stepped[0]


def weights_kernel(cc, kz, k):
    masks = coarse_masks()
    faces = [(cc[i] + cc[i + 1]) * (0.5 * COARSE_RATE) for i in range(7)]
    faces[2] = jnp.where(place()[1], faces[2], 0.0)
    faces[6] = jnp.where(place()[2], faces[6], 0.0)
    for i in range(7):
        kz[i] = faces[i]
    for i in range(6):
        for f, a in enumerate(coarse_weights(cc[i + 1], faces[i] + faces[i + 1], masks)):
            k[i, f] = a


def final_kernel(far, near, other, own_start, kz, k, spread, tall, lower, upper, out, made, sems):
    par, _, _, slice_at = place()

    def previous(p):
        return jnp.where(par == 1, near[p + 2], other[15 - p])

    def second(p):
        return jnp.where(par == 1, other[6 - p], far[p + 3])

    def first(p):
        return jnp.where(par == 1, far[p + 3], other[6 - p])

    def gate(level, a):
        return jnp.where(slice_at >= level, a, 0.0)

    def grow(d, lo, hi):
        return {
            p: coarse_step(d[p], d[p + 1], d[p - 1], kz[p + 3], kz[p + 2], [k[p + 2, i] for i in range(5)])
            for p in range(lo, hi)
        }

    d = {p: gate(3, first(p)) for p in range(-3, 5)}
    u = grow(d, -2, 4)
    d = {p: u[p] + gate(2, second(p)) for p in range(-2, 4)}
    u = grow(d, -1, 3)
    d = {p: gate(1, u[p] + previous(p) - own_start[p + 1]) for p in range(-1, 3)}
    u = grow(d, 0, 2)
    wide = split_dot(jnp.concatenate([u[0], u[1]], axis=0), spread[...])
    high = wide.astype(BF16)
    low = (wide - high.astype(F32)).astype(BF16)
    change = mxu(tall[...], high) + mxu(tall[...], low)
    copies = []
    for half, fine in ((0, lower), (1, upper)):

        @pl.loop(0, 4, unroll=True)
        def _(i):
            for side in range(2):
                for h in range(2):
                    rows = slice(32 * side, 32 * side + 32)
                    cut = change[32 * half : 32 * half + 32, 256 * side + LANES * h : 256 * side + LANES * (h + 1)]
                    made[half, half_plane(par, i), rows, LANES * h : LANES * (h + 1)] = fine[i, h, rows] + cut

        first = HALF * (par if half == 0 else 1 - par)
        copies.append(pltpu.make_async_copy(made.at[half], out.at[pl.ds(first, HALF)], sems.at[half]))
        copies[-1].start()
    for copy in copies:
        copy.wait()


def call(kernel, outs, scratch, flops, count):
    return pl.pallas_call(
        kernel,
        out_shape=[jax.ShapeDtypeStruct(s, F32) for s in outs],
        in_specs=[pl.BlockSpec(memory_space=pltpu.VMEM)] * count,
        out_specs=[pl.BlockSpec(memory_space=pltpu.VMEM)] * len(outs),
        scratch_shapes=[pltpu.VMEM(s, F32) for s in scratch],
        compiler_params=pltpu.CompilerParams(vmem_limit_bytes=VMEM_LIMIT),
        cost_estimate=pl.CostEstimate(flops=flops, bytes_accessed=flops // 4, transcendentals=0),
    )


def per_device(states, conductivity):
    return iteration(states[0], conductivity)[None]


def iteration(v, c):
    planes, rows, cols = v.shape
    plane = (rows, cols)
    wide, padded, block = (2, ROWS, LANES), (2, PADDED, LANES), (8, LANES)
    count, slices = lax.axis_size("space"), lax.axis_size("tm")

    slow_pairs = [(i, i + 1) for i in range(1, count - 1, 2)]
    slow_pairs += [(b, a) for a, b in slow_pairs]
    fast_pairs = [(i, i ^ 1) for i in range(count)]
    slow = lambda x: lax.ppermute(x, "space", slow_pairs)
    fast = lambda x: lax.ppermute(x, "space", fast_pairs)

    outs = [jax.ShapeDtypeStruct((2 * planes,) + plane, F32)]
    outs += [jax.ShapeDtypeStruct(m, BF16) for m in ((512, LANES), (LANES, 512), (64, 16))]
    whole, pool, spread, tall = pl.pallas_call(
        pack_kernel,
        out_shape=outs,
        in_specs=[pl.BlockSpec(memory_space=pltpu.HBM)] * 2,
        out_specs=[pl.BlockSpec(memory_space=pltpu.VMEM)] * 4,
        scratch_shapes=[pltpu.SemaphoreType.DMA((2,))],
        compiler_params=pltpu.CompilerParams(vmem_limit_bytes=VMEM_LIMIT),
    )(*(pltpu.with_memory_space_constraint(x, pltpu.HBM) for x in (v, c)))
    from_slow = slow(whole)
    from_fast = fast(whole)

    (own,) = call(coarse_kernel, [(4,) + block], [(8,) + padded] * 2, 1_000_000, 2)(whole, pool)
    theirs = fast(own)
    a, b, kz, kk, upper, end = call(
        early_kernel,
        [(12,) + padded, (12,) + padded, (11,) + wide, (11, 5) + wide, (4,) + wide, (1,) + block],
        [(12,) + padded],
        8_000_000,
        3,
    )(whole, from_fast, pool)
    mate_end = fast(end)
    (early,) = call(jump_kernel, [(5,) + block], [], 100_000, 4)(own, theirs, end, mate_end)
    beyond = slow(early)
    lower, jumps, before = call(
        late_kernel,
        [(4,) + wide, (2,) + block, (1,) + block],
        [(14,) + padded] * 3 + [(9, 5) + wide, (9,) + wide, (4,) + wide],
        8_000_000,
        8,
    )(whole, from_slow, a, b, kz, kk, pool, own)
    late = fast(jnp.concatenate([jumps, beyond[:3]]))

    line = jnp.stack(
        [beyond[1], beyond[0], jumps[1], jumps[0], early[0], early[1], late[0], late[1], late[2], late[3]]
    )

    def joined(x, steps):
        pairs = [(a * count + i, b * count + i) for i in range(count) for a, b in steps[i % 2]]
        return lax.ppermute(x, ("tm", "space"), pairs)

    far = joined(line, ([(i, i + 2) for i in range(slices - 2)], [(0, slices - 1)]))
    near = joined(line[1:9], ([], [(i, i + 1) for i in range(slices - 1)]))
    cc = jnp.stack([beyond[4], beyond[3], beyond[2], own[2], own[3], theirs[3], theirs[2], late[4]])
    ckz, ck = call(weights_kernel, [(7,) + block, (6, 5) + block], [], 100_000, 1)(cc)
    own_start = jnp.concatenate([before, own[:2], theirs[1:2]])
    other = fast(jnp.concatenate([far, near]))
    return pl.pallas_call(
        final_kernel,
        out_shape=jax.ShapeDtypeStruct((planes,) + plane, F32),
        in_specs=[pl.BlockSpec(memory_space=pltpu.VMEM)] * 10,
        out_specs=pl.BlockSpec(memory_space=pl.ANY),
        scratch_shapes=[pltpu.VMEM((2, HALF) + plane, F32), pltpu.SemaphoreType.DMA((2,))],
        compiler_params=pltpu.CompilerParams(vmem_limit_bytes=VMEM_LIMIT),
    )(far, near, other, own_start, ckz, ck, spread, tall, lower, upper)


def solution(mesh):
    return jax.shard_map(
        per_device,
        mesh=mesh,
        in_specs=(P("tm", "space", None, None), P("space", None, None)),
        out_specs=P("tm", "space", None, None),
        check_vma=False,
    )
```

```python
import jax
import jax.numpy as jnp
from jax import lax
from jax.experimental import pallas as pl
from jax.experimental.pallas import tpu as pltpu
from jax.sharding import PartitionSpec as P


FSTEPS = 4
COARSEN = 4
FINE_RATE = 0.1
COARSE_RATE = FINE_RATE * FSTEPS / 16.0
HALF = 4
F32 = jnp.float32
BF16 = jnp.bfloat16
VMEM_LIMIT = 24 * 1024 * 1024
LANES = 128
ROWS = 64
TOP = 8
PADDED = 80
UNROLL = True
CHUNK = 8


def place():
    k, count = lax.axis_index("space"), lax.axis_size("space")
    inside = lambda i: (i != 0) & (i != count - 1)
    par = k % 2
    return par, inside(k), inside(k + 1 - 2 * par), lax.axis_index("tm")


def own_plane(par, i):
    return i + par * (7 - 2 * i)


def half_plane(par, i):
    return i + par * (3 - 2 * i)


def slow_plane(par, i):
    return (7 - i) + par * (2 * i - 7)


def rows_of(ref, p, h, shift=0):
    return ref[p, h, TOP + shift : TOP + ROWS + shift, :]


def put(ref, p, plane):
    for h in range(2):
        ref[p, h, TOP : TOP + ROWS, :] = plane[:, h * LANES : (h + 1) * LANES]


def blank_margins(ref, planes):
    for p in range(planes):
        for h in range(2):
            ref[p, h, 0:TOP, :] = jnp.zeros((TOP, LANES), F32)
            ref[p, h, TOP + ROWS : PADDED, :] = jnp.zeros((TOP, LANES), F32)


def mirror_margins(ref, p):
    for h in range(2):
        ref[p, h, TOP - 1 : TOP, :] = -ref[p, h, TOP : TOP + 1, :]
        ref[p, h, TOP + ROWS : TOP + ROWS + 1, :] = -ref[p, h, TOP + ROWS - 1 : TOP + ROWS, :]


def lane_turns(a0, a1):
    at = lax.broadcasted_iota(jnp.int32, a0.shape, 1)
    up0, up1 = pltpu.roll(a0, LANES - 1, 1), pltpu.roll(a1, LANES - 1, 1)
    down0, down1 = pltpu.roll(a0, 1, 1), pltpu.roll(a1, 1, 1)
    return (jnp.where(at == LANES - 1, up1, up0), up1), (down0, jnp.where(at == 0, down0, down1)), at


def fill_faces(c, kz, lo, hi, scale, unroll):
    @pl.loop(lo, hi, unroll=unroll)
    def _(p):
        for h in range(2):
            kz[p, h] = (rows_of(c, p, h) + rows_of(c, p + 1, h)) * scale


def fill_coefficients(c, kz, k, lo, hi, scale, unroll):
    @pl.loop(lo, hi, unroll=unroll)
    def _(p):
        a0, a1 = rows_of(c, p, 0), rows_of(c, p, 1)
        (up0, up1), (down0, down1), at = lane_turns(a0, a1)
        up1 = jnp.where(at == LANES - 1, -a1, up1)
        down0 = jnp.where(at == 0, -a0, down0)
        for h, a, up, down in ((0, a0, up0, down0), (1, a1, up1, down1)):
            kxu = (a + rows_of(c, p, h, 1)) * scale
            kxd = (a + rows_of(c, p, h, -1)) * scale
            kyu = (a + up) * scale
            kyd = (a + down) * scale
            k[p, 0, h] = 1.0 - ((kxu + kxd) + (kyu + kyd) + (kz[p, h] + kz[p - 1, h]))
            k[p, 1, h] = kxu
            k[p, 2, h] = kxd
            k[p, 3, h] = kyu
            k[p, 4, h] = kyd


def advance(src, store, kz, k, lo, hi, unroll, shift=0):
    at = lax.broadcasted_iota(jnp.int32, (CHUNK, LANES), 1)

    def some(p):
        q = p - shift
        made = []
        for r in range(0, ROWS, CHUNK):
            cut = lambda ref, i, h, s=0: ref[i, h, TOP + r + s : TOP + r + s + CHUNK, :]
            w = lambda i, h: k[q, i, h, r : r + CHUNK, :]
            v = [cut(src, p, h) for h in range(2)]
            up = [pltpu.roll(v[h], LANES - 1, 1) for h in range(2)]
            down = [pltpu.roll(v[h], 1, 1) for h in range(2)]
            up = [jnp.where(at == LANES - 1, up[1], up[0]), up[1]]
            down = [down[0], jnp.where(at == 0, down[0], down[1])]
            for h in range(2):
                a = w(0, h) * v[h]
                b = kz[q, h, r : r + CHUNK] * cut(src, p + 1, h) + kz[q - 1, h, r : r + CHUNK] * cut(src, p - 1, h)
                d = w(1, h) * cut(src, p, h, 1) + w(2, h) * cut(src, p, h, -1)
                e = w(3, h) * up[h] + w(4, h) * down[h]
                made.append((r, h, (a + b) + (d + e)))
        return made

    @pl.loop(lo, hi, unroll=unroll)
    def _(p):
        for r, h, a in some(p):
            store(p, h, r, a)


def into(ref):
    def store(p, h, r, a):
        ref[p, h, TOP + r : TOP + r + CHUNK, :] = a

    return store


def into_fine(ref, shift):
    def store(p, h, r, a):
        ref[p - shift, h, r : r + CHUNK, :] = a

    return store


def block_sums(ref, first, top):
    parts = []
    for side in range(2):
        for h in range(2):
            total = None
            for p in range(first, first + COARSEN):
                for r in range(COARSEN):
                    term = ref[p, h, pl.ds(top + 32 * side + r, 8, stride=COARSEN), :]
                    total = term if total is None else total + term
            parts.append(total)
    return jnp.concatenate(parts, axis=1)


def mxu(a, b):
    return lax.dot_general(a, b, (((1,), (0,)), ((), ())), preferred_element_type=F32)


def split_dot(a, b):
    high = a.astype(BF16)
    low = (a - high.astype(F32)).astype(BF16)
    return mxu(high, b) + mxu(low, b)


def pooled(sums, pool):
    return split_dot(sums, pool) * (1.0 / COARSEN**3)


def matches(rows, cols, by_row):
    r = lax.broadcasted_iota(jnp.int32, (rows, cols), 0)
    c = lax.broadcasted_iota(jnp.int32, (rows, cols), 1)
    same = r // COARSEN == c if by_row else c // COARSEN == r
    return jnp.where(same, 1.0, 0.0).astype(BF16)


def pack_kernel(v, c, whole, pool, spread, tall, sems):
    copies = [
        pltpu.make_async_copy(src, whole.at[pl.ds(f * 8, 8)], sems.at[f]) for f, src in enumerate((v, c))
    ]
    for copy in copies:
        copy.start()
    pool[...] = matches(*pool.shape, True)
    spread[...] = matches(*spread.shape, False)
    tall[...] = matches(*tall.shape, True)
    for copy in copies:
        copy.wait()


def put_own(par, whole, field, coefficient):
    @pl.loop(0, 8)
    def _(i):
        put(field, i, whole[own_plane(par, i)])
        put(coefficient, i, whole[8 + own_plane(par, i)])


def coarse_kernel(whole, pool, out, v0, c0):
    put_own(place()[0], whole, v0, c0)
    sums = [block_sums(ref, 4 * b, TOP) for ref in (v0, c0) for b in range(2)]
    res = pooled(jnp.concatenate(sums, axis=0), pool[...])
    for i in range(4):
        out[i] = res[8 * i : 8 * i + 8]


def early_kernel(whole, h, pool, a, b, kz, k, fine, end, c0):
    par = place()[0]
    blank_margins(a, 12)
    blank_margins(b, 12)
    put_own(par, whole, a, c0)

    @pl.loop(0, 4)
    def _(i):
        put(a, 8 + i, h[own_plane(par, i)])
        put(c0, 8 + i, h[8 + own_plane(par, i)])

    for i in range(12):
        mirror_margins(c0, i)
    scale = 0.5 * FINE_RATE
    fill_faces(c0, kz, 0, 11, scale, UNROLL)
    fill_coefficients(c0, kz, k, 1, 11, scale, UNROLL)
    advance(a, into(b), kz, k, 1, 11, UNROLL)
    advance(b, into(a), kz, k, 2, 10, UNROLL)
    advance(a, into(b), kz, k, 3, 9, UNROLL)
    advance(b, into_fine(fine, 4), kz, k, 4, 8, UNROLL)
    end[0] = pooled(block_sums(fine, 0, 0), pool[...])


def row_turns(a):
    other = pltpu.roll(a, LANES // 2, 1)
    row = lax.broadcasted_iota(jnp.int32, a.shape, 0)
    up = jnp.where(row == 7, pltpu.roll(other, 7, 0), pltpu.roll(a, 7, 0))
    down = jnp.where(row == 0, pltpu.roll(other, 1, 0), pltpu.roll(a, 1, 0))
    return up, down


def coarse_masks():
    scale = 0.5 * COARSE_RATE
    row = lax.broadcasted_iota(jnp.int32, (8, LANES), 0)
    lane = lax.broadcasted_iota(jnp.int32, (8, LANES), 1)
    left = lane < LANES // 2
    up = jnp.where(left | (row < 7), scale, 0.0)
    down = jnp.where(left & (row == 0), 0.0, scale)
    right = jnp.where(lane % (LANES // 2) == LANES // 2 - 1, 0.0, scale)
    before = jnp.where(lane % (LANES // 2) == 0, 0.0, scale)
    return up, down, right, before


def coarse_weights(c, faces, masks):
    up, down = row_turns(c)
    kxu, kxd = (c + up) * masks[0], (c + down) * masks[1]
    kyu = (c + pltpu.roll(c, LANES - 1, 1)) * masks[2]
    kyd = (c + pltpu.roll(c, 1, 1)) * masks[3]
    return 1.0 - ((kxu + kxd) + (kyu + kyd) + faces), kxu, kxd, kyu, kyd


def coarse_step(v, above, below, face_above, face_below, w):
    up, down = row_turns(v)
    x = w[1] * up + w[2] * down
    y = w[3] * pltpu.roll(v, LANES - 1, 1) + w[4] * pltpu.roll(v, 1, 1)
    return (w[0] * v + (face_above * above + face_below * below)) + (x + y)


def coarse_change(start, cc, faces, i, masks):
    w = coarse_weights(cc[i], faces[i] + faces[i - 1], masks)
    step = coarse_step(start[i], start[i + 1], start[i - 1], faces[i], faces[i - 1], w)
    return jnp.where(place()[3] > 0, step, 0.0)


def jump_kernel(own, theirs, end, mate_end, out):
    start = [own[0], own[1], theirs[1], theirs[0]]
    cc = [own[2], own[3], theirs[3], theirs[2]]
    faces = [(cc[i] + cc[i + 1]) * (0.5 * COARSE_RATE) for i in range(3)]
    masks = coarse_masks()
    out[0] = end[0] - coarse_change(start, cc, faces, 1, masks)
    out[1] = mate_end[0] - coarse_change(start, cc, faces, 2, masks)
    for i in range(3):
        out[2 + i] = cc[i]


def late_kernel(whole, g, a, b, kz, k, pool, own, fine, out, before, v0, c0, w0, kl, kzl, extra):
    par, slow_ok, _, _ = place()
    blank_margins(v0, 14)
    blank_margins(w0, 14)

    @pl.loop(0, 8, unroll=True)
    def _(i):
        put(v0, 7 - i, g[slow_plane(par, i)])
        put(c0, 7 - i, g[8 + slow_plane(par, i)])

    for i in range(2):
        put(v0, 8 + i, whole[own_plane(par, i)])
        put(c0, 8 + i, whole[8 + own_plane(par, i)])
    for i in range(10):
        mirror_margins(c0, i)
    sums = [block_sums(ref, 4 * q, TOP) for ref in (v0, c0) for q in range(2)]
    beyond = pooled(jnp.concatenate(sums, axis=0), pool[...])
    start = [beyond[:8], beyond[8:16], own[0], own[1]]
    cc = [beyond[16:24], beyond[24:], own[2], own[3]]
    faces = [(cc[i] + cc[i + 1]) * (0.5 * COARSE_RATE) for i in range(3)]
    faces[1] = jnp.where(slow_ok, faces[1], 0.0)
    masks = coarse_masks()
    before[0] = start[1]
    stepped = [coarse_change(start, cc, faces, i, masks) for i in (1, 2)]
    scale = 0.5 * FINE_RATE
    fill_faces(c0, kzl, 0, 9, scale, True)
    for h in range(2):
        kzl[7, h] = jnp.where(slow_ok, kzl[7, h], 0.0)
    fill_coefficients(c0, kzl, kl, 1, 9, scale, True)
    advance(v0, into(w0), kzl, kl, 1, 9, True)
    for h in range(2):
        w0[9, h] = b[1, h]
        w0[10, h] = b[2, h]
    advance(w0, into(v0), kzl, kl, 2, 9, True)
    advance(w0, into(v0), kz, k, 9, 10, True, 8)
    for h in range(2):
        v0[10, h] = a[2, h]
        v0[11, h] = a[3, h]
    advance(v0, into(w0), kzl, kl, 3, 9, True)
    advance(v0, into(w0), kz, k, 9, 11, True, 8)
    for h in range(2):
        w0[11, h] = b[3, h]
        w0[12, h] = b[4, h]
    advance(w0, into_fine(extra, 4), kzl, kl, 4, 8, True)
    advance(w0, into_fine(fine, 8), kzl, kl, 8, 9, True)
    advance(w0, into_fine(fine, 8), kz, k, 9, 12, True, 8)
    ends = pooled(jnp.concatenate([block_sums(ref, 0, 0) for ref in (extra, fine)], axis=0), pool[...])
    out[0] = ends[8:] - stepped[1]
    out[1] = ends[:8] - stepped[0]


def weights_kernel(cc, kz, k):
    masks = coarse_masks()
    faces = [(cc[i] + cc[i + 1]) * (0.5 * COARSE_RATE) for i in range(7)]
    faces[2] = jnp.where(place()[1], faces[2], 0.0)
    faces[6] = jnp.where(place()[2], faces[6], 0.0)
    for i in range(7):
        kz[i] = faces[i]
    for i in range(6):
        for f, a in enumerate(coarse_weights(cc[i + 1], faces[i] + faces[i + 1], masks)):
            k[i, f] = a


def final_kernel(far, near, other, own_start, kz, k, spread, tall, lower, upper, out, made, sems):
    par, _, _, slice_at = place()

    def previous(p):
        return jnp.where(par == 1, near[p + 2], other[15 - p])

    def second(p):
        return jnp.where(par == 1, other[6 - p], far[p + 3])

    def first(p):
        return jnp.where(par == 1, far[p + 3], other[6 - p])

    def gate(level, a):
        return jnp.where(slice_at >= level, a, 0.0)

    def grow(d, lo, hi):
        return {
            p: coarse_step(d[p], d[p + 1], d[p - 1], kz[p + 3], kz[p + 2], [k[p + 2, i] for i in range(5)])
            for p in range(lo, hi)
        }

    d = {p: gate(3, first(p)) for p in range(-3, 5)}
    u = grow(d, -2, 4)
    d = {p: u[p] + gate(2, second(p)) for p in range(-2, 4)}
    u = grow(d, -1, 3)
    d = {p: gate(1, u[p] + previous(p) - own_start[p + 1]) for p in range(-1, 3)}
    u = grow(d, 0, 2)
    wide = split_dot(jnp.concatenate([u[0], u[1]], axis=0), spread[...])
    high = wide.astype(BF16)
    low = (wide - high.astype(F32)).astype(BF16)
    change = mxu(tall[...], high) + mxu(tall[...], low)
    copies = []
    for half, fine in ((0, lower), (1, upper)):
        first = HALF * (par if half == 0 else 1 - par)
        for i in range(HALF):
            at_plane = half_plane(par, i)
            for side in range(2):
                for h in range(2):
                    rows = slice(32 * side, 32 * side + 32)
                    cut = change[32 * half : 32 * half + 32, 256 * side + LANES * h : 256 * side + LANES * (h + 1)]
                    made[half, i, rows, LANES * h : LANES * (h + 1)] = fine[i, h, rows] + cut
            copies.append(
                pltpu.make_async_copy(made.at[half, i], out.at[first + at_plane], sems.at[HALF * half + i])
            )
            copies[-1].start()
    for copy in copies:
        copy.wait()


def call(kernel, outs, scratch, flops, count):
    return pl.pallas_call(
        kernel,
        out_shape=[jax.ShapeDtypeStruct(s, F32) for s in outs],
        in_specs=[pl.BlockSpec(memory_space=pltpu.VMEM)] * count,
        out_specs=[pl.BlockSpec(memory_space=pltpu.VMEM)] * len(outs),
        scratch_shapes=[pltpu.VMEM(s, F32) for s in scratch],
        compiler_params=pltpu.CompilerParams(vmem_limit_bytes=VMEM_LIMIT),
        cost_estimate=pl.CostEstimate(flops=flops, bytes_accessed=flops // 4, transcendentals=0),
    )


def per_device(states, conductivity):
    return iteration(states[0], conductivity)[None]


def iteration(v, c):
    planes, rows, cols = v.shape
    plane = (rows, cols)
    wide, padded, block = (2, ROWS, LANES), (2, PADDED, LANES), (8, LANES)
    count, slices = lax.axis_size("space"), lax.axis_size("tm")

    slow_pairs = [(i, i + 1) for i in range(1, count - 1, 2)]
    slow_pairs += [(b, a) for a, b in slow_pairs]
    fast_pairs = [(i, i ^ 1) for i in range(count)]
    slow = lambda x: lax.ppermute(x, "space", slow_pairs)
    fast = lambda x: lax.ppermute(x, "space", fast_pairs)

    outs = [jax.ShapeDtypeStruct((2 * planes,) + plane, F32)]
    outs += [jax.ShapeDtypeStruct(m, BF16) for m in ((512, LANES), (LANES, 512), (64, 16))]
    whole, pool, spread, tall = pl.pallas_call(
        pack_kernel,
        out_shape=outs,
        in_specs=[pl.BlockSpec(memory_space=pltpu.HBM)] * 2,
        out_specs=[pl.BlockSpec(memory_space=pltpu.VMEM)] * 4,
        scratch_shapes=[pltpu.SemaphoreType.DMA((2,))],
        compiler_params=pltpu.CompilerParams(vmem_limit_bytes=VMEM_LIMIT),
    )(*(pltpu.with_memory_space_constraint(x, pltpu.HBM) for x in (v, c)))
    from_slow = slow(whole)
    from_fast = fast(whole)

    (own,) = call(coarse_kernel, [(4,) + block], [(8,) + padded] * 2, 1_000_000, 2)(whole, pool)
    theirs = fast(own)
    a, b, kz, kk, upper, end = call(
        early_kernel,
        [(12,) + padded, (12,) + padded, (11,) + wide, (11, 5) + wide, (4,) + wide, (1,) + block],
        [(12,) + padded],
        8_000_000,
        3,
    )(whole, from_fast, pool)
    mate_end = fast(end)
    (early,) = call(jump_kernel, [(5,) + block], [], 100_000, 4)(own, theirs, end, mate_end)
    beyond = slow(early)
    lower, jumps, before = call(
        late_kernel,
        [(4,) + wide, (2,) + block, (1,) + block],
        [(14,) + padded] * 3 + [(9, 5) + wide, (9,) + wide, (4,) + wide],
        8_000_000,
        8,
    )(whole, from_slow, a, b, kz, kk, pool, own)
    late = fast(jnp.concatenate([jumps, beyond[:3]]))

    line = jnp.stack(
        [beyond[1], beyond[0], jumps[1], jumps[0], early[0], early[1], late[0], late[1], late[2], late[3]]
    )

    def joined(x, steps):
        pairs = [(a * count + i, b * count + i) for i in range(count) for a, b in steps[i % 2]]
        return lax.ppermute(x, ("tm", "space"), pairs)

    far = joined(line, ([(i, i + 2) for i in range(slices - 2)], [(0, slices - 1)]))
    near = joined(line[1:9], ([], [(i, i + 1) for i in range(slices - 1)]))
    cc = jnp.stack([beyond[4], beyond[3], beyond[2], own[2], own[3], theirs[3], theirs[2], late[4]])
    ckz, ck = call(weights_kernel, [(7,) + block, (6, 5) + block], [], 100_000, 1)(cc)
    own_start = jnp.concatenate([before, own[:2], theirs[1:2]])
    other = fast(jnp.concatenate([far, near]))
    return pl.pallas_call(
        final_kernel,
        out_shape=jax.ShapeDtypeStruct((planes,) + plane, F32),
        in_specs=[pl.BlockSpec(memory_space=pltpu.VMEM)] * 10,
        out_specs=pl.BlockSpec(memory_space=pl.ANY),
        scratch_shapes=[pltpu.VMEM((2, HALF) + plane, F32), pltpu.SemaphoreType.DMA((2 * HALF,))],
        compiler_params=pltpu.CompilerParams(vmem_limit_bytes=VMEM_LIMIT),
    )(far, near, other, own_start, ckz, ck, spread, tall, lower, upper)


def solution(mesh):
    return jax.shard_map(
        per_device,
        mesh=mesh,
        in_specs=(P("tm", "space", None, None), P("space", None, None)),
        out_specs=P("tm", "space", None, None),
        check_vma=False,
    )
```
